32 devices in a mesh: group: 4 (over y, core), expert: 8 (over z, x).
Axes of the slice: x: 2, y: 2, z: 4, core: 2. Of those that a mesh axis runs over, the one named last changes fastest.
Arguments:
- tokens: bfloat16 [1024, 2048], P(('group', 'expert')), may hold values from -6 to 6
- out_grad: bfloat16 [1024, 2048], P(('group', 'expert')), may hold values from -6 to 6
- expert_ids: int32 [1024, 4], P(('group', 'expert')), may hold values from 0 to 63, as said below
- gate_w: bfloat16 [1024, 4], P(('group', 'expert')), may hold values from 0.049804688 to 0.59765625
- query_ids: int32 [32, 32], P(('group', 'expert')), may hold values from 0 to 7, never falling along the last dimension, each value on 1 to 8 neighbouring positions
- w_gate: bfloat16 [64, 2048, 512], P(('group', 'expert')), may hold values from -0.125 to 0.125
- w_up: bfloat16 [64, 2048, 512], P(('group', 'expert')), may hold values from -0.125 to 0.125
- w_down: bfloat16 [64, 512, 2048], P(('group', 'expert')), may hold values from -0.25 to 0.25
- proj_out: bfloat16 [64, 2048, 64], P(('group', 'expert')), may hold values from -0.125 to 0.125
- proj_in: bfloat16 [64, 512, 64], P(('group', 'expert')), may hold values from -0.25 to 0.25
- train_grads: bfloat16 [64, 4096, 512], P(('group', 'expert')), may hold values from -0.09375 to 0.09375
Outputs:
- token_grads: bfloat16 [1024, 2048], P(('group', 'expert'))
- scores: float32 [256, 512], P(('group', 'expert'))
The draws below stay inside these ranges and needn't reach their ends.
Inputs may be any that keep to these rules, and one draw needn't show every extreme that they name: `expert_ids`: each token names 4 different experts, two in each of 2 different groups, a group being 16 consecutive experts. Among the 32 tokens of one block every group is named by exactly 16 tokens and every expert by at most 4 tokens; in every block some expert is named by exactly 4. `query_ids`: along one block's tokens the query number never falls; each of the 8 queries of a block has 1 to 8 tokens, and one has exactly 8.
All inputs are finite; a program needn't handle non-finite values.
Results may differ from the reference program's by a relative error of at most 0.0064.
Values may be sent and summed in bfloat16 or wider, within the bound.
No kernel may reach another device: no remote copies, remote signals or barrier semaphores. Data moves between devices by JAX's collectives and lax.ppermute only.
A program may use at most 128 MiB of HBM per device.

```python
import math
import jax
import jax.numpy as jnp
import numpy as np
from jax import lax

D = 2048
F = 512
RANK = 64
TRAIN = 512
TOK_DEV = 32
QRY_DEV = 8
GROUPS = 4
EXP_GROUP = 16
EXPERTS = 64
GROUP_TOP = 2
TOP = 4
CAP = 4
BLOCKS = 32
TOKENS = 1024
QUERIES = 256
QMOST = 8


def draw_expert_ids(key, part):
    blocks = TOKENS // TOK_DEV
    hot_count = EXP_GROUP // 4
    key_list = jax.random.split(key, 5)
    position = jax.vmap(lambda key_one: jax.random.permutation(key_one, TOK_DEV))(jax.random.split(key_list[0], blocks))
    group_perm = jax.vmap(lambda key_one: jax.random.permutation(key_one, GROUPS))(jax.random.split(key_list[1], blocks))
    local_perm = jax.vmap(lambda key_one: jax.random.permutation(key_one, EXP_GROUP))(jax.random.split(key_list[2], GROUPS))
    spread = jax.random.randint(key_list[3], (blocks, 1), 2 * hot_count, EXP_GROUP - hot_count + 1)
    offset = jax.random.randint(key_list[4], (blocks, 1), 0, EXP_GROUP)
    parity = position % 2
    half_pos = position // 2
    choose = (parity[:, :, None] + 2 * jnp.arange(GROUP_TOP)[None, None, :]) % GROUPS
    group_ids = jnp.take_along_axis(jnp.broadcast_to(group_perm[:, None, :], (blocks, TOK_DEV, GROUPS)), choose, axis=2)
    first_local = half_pos % hot_count
    second_local = hot_count + (half_pos + offset) % spread
    first_expert = local_perm[group_ids, first_local[:, :, None]]
    second_expert = local_perm[group_ids, second_local[:, :, None]]
    experts = group_ids[:, :, :, None] * EXP_GROUP + jnp.stack([first_expert, second_expert], axis=3)
    return experts.reshape(TOKENS, TOP).astype(jnp.int32)


def level_of(key, extent, shards, smallest, high):
    loudness = 1.0
    for dim, parts in shards:
        draws = jax.random.uniform(jax.random.fold_in(jax.random.fold_in(key, 6), dim), (parts,), jnp.float32, smallest / len(shards), high / len(shards))
        loudness = loudness * jnp.repeat(jnp.exp(draws), extent[dim] // parts).reshape((-1,) + (1,) * (len(extent) - 1 - dim))
    return loudness


def length_profile(count, total, most, slope):
    weights = [(1 << 20) // math.isqrt(standing ** slope) + 1 for standing in range(2, count + 1)]
    surplus, holding = total - most - (count - 1), [1] * (count - 1)
    while surplus > 0:
        free = [i for i in range(count - 1) if holding[i] < most]
        mass, budget = sum([weights[i] for i in free]), surplus
        for i in free:
            more = min(most - holding[i], max(1, budget * weights[i] // mass), surplus)
            holding[i] = holding[i] + more
            surplus = surplus - more
    return np.array([most] + holding)


def ragged_sizes(rng, count, total, bound, lean):
    if count == 2:
        one = jax.random.randint(rng, (), max(1, total - bound), min(bound, total - 1) + 1)
        return jnp.stack([one, total - one])
    sizes = jnp.asarray(length_profile(count, total, bound, lean), jnp.int32)
    couples = (count - 1) // 2
    source_of, taker = sizes[1:1 + 2 * couples:2], sizes[2:2 + 2 * couples:2]
    room = jnp.minimum(source_of - 1, bound - taker)
    shifted = jax.random.randint(jax.random.fold_in(rng, 1), (couples,), 0, 1 << 20) % (room + 1)
    sizes = sizes.at[1:1 + 2 * couples:2].set(source_of - shifted).at[2:2 + 2 * couples:2].set(taker + shifted)
    return sizes[jax.random.permutation(jax.random.fold_in(rng, 2), count)]


def centred(own_key, dims, scale, limit, cuts=(), kind=jnp.bfloat16):
    factor_of = level_of(own_key, dims, cuts, -0.22, 0.18) if cuts else 1.0
    entries = jax.random.normal(own_key, dims, jnp.float32) * scale * factor_of
    return jnp.minimum(jnp.maximum(entries, -limit), limit).astype(kind)


def setup_inputs(seed: int = 0) -> dict:
    key_of = jax.random.split(jax.random.key(seed), 12)
    tokens = centred(key_of[0], (TOKENS, D), 1.0, 6.0, ((0, 32),))
    out_grad = centred(key_of[1], (TOKENS, D), 1.0, 6.0, ((0, 32),))
    expert_ids = draw_expert_ids(jax.random.fold_in(key_of[11], 71), 0)
    gate_w = jnp.clip(0.049804688 + 0.54785156 * jax.random.uniform(key_of[3], (TOKENS, TOP), jnp.float32) ** level_of(key_of[3], (TOKENS, TOP), ((0, 32),), -0.2, 0.2), 0.049804688, 0.59765625).astype(jnp.bfloat16)
    query_ids = jax.vmap(lambda own: jnp.searchsorted(jnp.cumsum(ragged_sizes(own, QRY_DEV, TOK_DEV, QMOST, 2)), jnp.arange(TOK_DEV), side="right"))(jax.random.split(key_of[4], BLOCKS)).reshape((BLOCKS, TOK_DEV)).astype(jnp.int32)
    w_gate = centred(key_of[5], (EXPERTS, D, F), D ** -0.5, 0.125, ((0, 32),))
    w_up = centred(key_of[6], (EXPERTS, D, F), D ** -0.5, 0.125, ((0, 32),))
    w_down = centred(key_of[7], (EXPERTS, F, D), F ** -0.5, 0.25, ((0, 32),))
    proj_out = centred(key_of[8], (EXPERTS, D, RANK), D ** -0.5, 0.125, ((0, 32),))
    proj_in = centred(key_of[9], (EXPERTS, F, RANK), F ** -0.5, 0.25, ((0, 32),))
    train_grads = centred(key_of[10], (EXPERTS, RANK * RANK, TRAIN), (RANK * RANK) ** -0.5, 0.09375, ((0, 32),))
    return {"tokens": tokens, "out_grad": out_grad, "expert_ids": expert_ids, "gate_w": gate_w, "query_ids": query_ids, "w_gate": w_gate, "w_up": w_up, "w_down": w_down, "proj_out": proj_out, "proj_in": proj_in, "train_grads": train_grads}


def pair_terms(rows_x, rows_g, rows_w, gate_mat, up_mat, down_mat, left_proj, right_proj, stored):
    contract = (((1,), (1,)), ((), ()))
    a_gate = jnp.dot(rows_x, gate_mat, preferred_element_type=jnp.float32)
    a_up = jnp.dot(rows_x, up_mat, preferred_element_type=jnp.float32)
    sigmoid_val = jax.nn.sigmoid(a_gate)
    active = a_gate * sigmoid_val
    hidden = (active * a_up).astype(jnp.bfloat16)
    delta_rows = (rows_w.astype(jnp.float32)[:, None] * rows_g.astype(jnp.float32)).astype(jnp.bfloat16)
    d_hidden = lax.dot_general(delta_rows, down_mat, contract, preferred_element_type=jnp.float32)
    grad_up = (d_hidden * active).astype(jnp.bfloat16)
    grad_gate = (d_hidden * a_up * sigmoid_val * (1.0 + a_gate * (1.0 - sigmoid_val))).astype(jnp.bfloat16)
    pair_grad = lax.dot_general(grad_gate, gate_mat, contract, preferred_element_type=jnp.float32)
    pair_grad = pair_grad + lax.dot_general(grad_up, up_mat, contract, preferred_element_type=jnp.float32)
    left_vec = jnp.dot(delta_rows, left_proj, preferred_element_type=jnp.float32)
    right_vec = jnp.dot(hidden, right_proj, preferred_element_type=jnp.float32)
    outer_prod = (left_vec[:, :, None] * right_vec[:, None, :]).reshape(left_vec.shape[0], -1).astype(jnp.bfloat16)
    pair_score = jnp.dot(outer_prod, stored, preferred_element_type=jnp.float32)
    return pair_grad.astype(jnp.bfloat16), pair_score


def reference(tokens, out_grad, expert_ids, gate_w, query_ids, w_gate, w_up, w_down, proj_out, proj_in, train_grads):
    pair_total = TOKENS * TOP
    flat_experts = expert_ids.reshape(-1).astype(jnp.int32)
    sorting = jnp.argsort(flat_experts, stable=True).astype(jnp.int32)
    counts = jnp.zeros((EXPERTS,), jnp.int32).at[flat_experts].add(1)
    starts = (jnp.cumsum(counts) - counts).astype(jnp.int32)
    room = BLOCKS * CAP
    flat_weights = gate_w.reshape(-1)

    def expert_step(carried, expert):
        grad_sum, score_sum = carried
        offsets = jnp.arange(room, dtype=jnp.int32)
        used = offsets < counts[expert]
        pair_index = sorting[jnp.minimum(starts[expert] + offsets, pair_total - 1)]
        token_index = (pair_index // TOP).astype(jnp.int32)
        rows_w = jnp.where(used, flat_weights[pair_index], jnp.zeros((), flat_weights.dtype))
        pair_grad, pair_score = pair_terms(tokens[token_index], out_grad[token_index], rows_w, w_gate[expert], w_up[expert], w_down[expert], proj_out[expert], proj_in[expert], train_grads[expert])
        grad_sum = grad_sum.at[token_index].add(pair_grad.astype(jnp.float32))
        score_sum = score_sum.at[token_index].add(pair_score)
        return (grad_sum, score_sum), None

    initial = (jnp.zeros((TOKENS, D), jnp.float32), jnp.zeros((TOKENS, TRAIN), jnp.float32))
    (grad_sum, score_sum), _ = lax.scan(expert_step, initial, jnp.arange(EXPERTS, dtype=jnp.int32))
    block_of = (jnp.arange(TOKENS, dtype=jnp.int32) // TOK_DEV).astype(jnp.int32)
    query_global = (block_of * QRY_DEV + query_ids.reshape(-1)).astype(jnp.int32)
    scores = jax.ops.segment_sum(score_sum, query_global, num_segments=QUERIES)
    return grad_sum.astype(jnp.bfloat16), scores
```

```python
import functools

import jax
import jax.numpy as jnp
from jax import lax
from jax.experimental import pallas as pl
from jax.experimental.pallas import tpu as pltpu
from jax.sharding import Mesh, PartitionSpec as P

QRY_DEV = 8
HALVES = 2
LANES = 128
F32 = jnp.float32
BF16 = jnp.bfloat16
NT = (((1,), (1,)), ((), ()))


def dot(a, b):
    return jnp.dot(a, b, preferred_element_type=F32)


def slot_masks(meta, half, sizes):
    tok, top, rows, span, capacity = sizes
    shape = (tok, rows)
    slot = lax.broadcasted_iota(jnp.int32, shape, 1)
    rank = (slot % capacity).astype(F32)
    expert = (slot // (span * capacity)) * (HALVES * span) + half * span + slot // capacity % span
    expert = expert.astype(F32)
    named = jnp.zeros(shape, F32)
    weight = jnp.zeros(shape, F32)
    for k in range(top):
        hit = jnp.where(meta[:, k : k + 1] == expert, 1.0, 0.0)
        named = named + hit
        weight = weight + hit * meta[:, top + k : top + k + 1]
    row = lax.broadcasted_iota(jnp.int32, (tok, tok), 0)
    col = lax.broadcasted_iota(jnp.int32, (tok, tok), 1)
    earlier = dot(jnp.where(col < row, 1.0, 0.0).astype(BF16), named.astype(BF16))
    place = jnp.where(earlier == rank, named, 0.0)
    return place, place * weight


def fill_slots(place, weighted, x, g, send_ref, place_ref):
    width = x.shape[1]
    place_ref[...] = place.astype(BF16)
    pick = place.T.astype(BF16)
    scale = jnp.sum(weighted.T, axis=1, keepdims=True)
    send_ref[:, :width] = dot(pick, x).astype(BF16)
    send_ref[:, width:] = (scale * dot(pick, g)).astype(BF16)


def own_kernel(sizes, half_ref, ids_ref, w_ref, x_ref, g_ref, pay_ref, send_ref, place_ref):
    tok, top = sizes[:2]
    width = x_ref.shape[1]
    flat = jnp.concatenate([ids_ref[...].astype(F32), w_ref[...].astype(F32)], axis=0)
    flat = jnp.concatenate([flat, jnp.zeros((LANES - 2 * top, tok), F32)], axis=0)
    flat = jnp.concatenate([flat, jnp.zeros((LANES, LANES - tok), F32)], axis=1)
    meta = flat.T[:tok, :]
    pay_ref[:, :width] = x_ref[...]
    pay_ref[:, width : 2 * width] = g_ref[...]
    pay_ref[:, 2 * width :] = meta.astype(BF16)
    place, weighted = slot_masks(meta, half_ref[0], sizes)
    fill_slots(place, weighted, x_ref[...], g_ref[...], send_ref, place_ref)


def guest_kernel(sizes, half_ref, pay_ref, send_ref, place_ref):
    width = send_ref.shape[1] // 2
    meta = pay_ref[:, 2 * width :].astype(F32)
    place, weighted = slot_masks(meta, half_ref[0], sizes)
    fill_slots(
        place, weighted, pay_ref[:, :width], pay_ref[:, width : 2 * width], send_ref, place_ref
    )


def expert_kernel(capacity, rows_ref, *refs):
    hbm, out_ref, vmem, outer_ref, sem = refs[:6], refs[6], refs[7:13], refs[13], refs[14]
    experts, width, hidden_width = hbm[0].shape
    rank = hbm[3].shape[2]
    rows = rows_ref.shape[0]
    order = (0, 1, 2, 3, 4, 5)

    def copy(i, j):
        return pltpu.make_async_copy(hbm[i].at[j], vmem[i].at[j], sem.at[i, j])

    for j in range(experts):
        for i in (0, 1, 2, 3, 4):
            copy(i, j).start()
    for j in range(experts):
        copy(5, j).start()
    gate, up, down, left_proj, right_proj, stored = vmem
    x = rows_ref[:, :width]
    delta = rows_ref[:, width:]
    owner = lax.broadcasted_iota(jnp.int32, (rows, 1), 0) // capacity % experts
    left = jnp.zeros((rows, rank), F32)
    right = jnp.zeros((rows, rank), F32)
    grad = jnp.zeros((rows, width), F32)
    for j in range(experts):
        mine = owner == j
        copy(0, j).wait()
        a_gate = dot(x, gate[j])
        copy(1, j).wait()
        a_up = dot(x, up[j])
        copy(2, j).wait()
        d_hidden = lax.dot_general(delta, down[j], NT, preferred_element_type=F32)
        sig = jax.nn.sigmoid(a_gate)
        active = a_gate * sig
        hidden = (active * a_up).astype(BF16)
        grad_up = jnp.where(mine, d_hidden * active, 0.0).astype(BF16)
        grad_gate = jnp.where(
            mine, d_hidden * a_up * sig * (1.0 + a_gate * (1.0 - sig)), 0.0
        ).astype(BF16)
        grad = grad + lax.dot_general(grad_gate, gate[j], NT, preferred_element_type=F32)
        grad = grad + lax.dot_general(grad_up, up[j], NT, preferred_element_type=F32)
        copy(3, j).wait()
        left = jnp.where(mine, dot(delta, left_proj[j]), left)
        copy(4, j).wait()
        right = jnp.where(mine, dot(hidden, right_proj[j]), right)
    out_ref[:, :width] = grad.astype(BF16)
    per = LANES // rank
    wide = jnp.concatenate([right] * per, axis=1)
    lane = lax.broadcasted_iota(jnp.int32, (rows, LANES), 1) // rank
    for c in range(rank // per):
        factor = left[:, c * per : c * per + 1]
        for k in range(1, per):
            factor = jnp.where(lane == k, left[:, c * per + k : c * per + k + 1], factor)
        outer = factor * wide
        for j in range(experts):
            outer_ref[j, :, c * LANES : (c + 1) * LANES] = jnp.where(owner == j, outer, 0.0).astype(
                BF16
            )
    score = jnp.zeros((rows, stored.shape[2]), F32)
    for j in range(experts):
        copy(5, j).wait()
        score = score + dot(outer_ref[j], stored[j])
    out_ref[:, width:] = score.astype(BF16)


def part_kernel(place_ref, rows_ref, out_ref):
    out_ref[...] = dot(place_ref[...], rows_ref[...]).astype(BF16)


def final_kernel(place_ref, rows_ref, part_ref, query_ref, grad_ref, score_ref):
    width = grad_ref.shape[1]
    total = dot(place_ref[...], rows_ref[...]) + part_ref[...].astype(F32)
    grad_ref[...] = total[:, :width].astype(BF16)
    wanted = lax.broadcasted_iota(jnp.int32, (score_ref.shape[0], query_ref.shape[1]), 0)
    pick = jnp.where(query_ref[...] == wanted, 1.0, 0.0)
    score_ref[...] = jnp.dot(
        pick, total[:, width:], precision=lax.Precision.HIGHEST, preferred_element_type=F32
    )


VMEM = pl.BlockSpec(memory_space=pltpu.VMEM)
SMEM = pl.BlockSpec(memory_space=pltpu.SMEM)
ANY = pl.BlockSpec(memory_space=pl.ANY)


def call(kernel, outs, in_specs, args, scratch=(), flops=1_000_000, moved=1_000_000, limit=None):
    return pl.pallas_call(
        kernel,
        out_shape=outs,
        in_specs=in_specs,
        out_specs=jax.tree.map(lambda _: VMEM, outs),
        scratch_shapes=scratch,
        compiler_params=pltpu.CompilerParams(vmem_limit_bytes=limit),
        cost_estimate=pl.CostEstimate(flops=flops, bytes_accessed=moved, transcendentals=0),
    )(*args)


def body(tokens, out_grad, expert_ids, gate_w, query_ids, *weights):
    tok, width = tokens.shape
    top = expert_ids.shape[1]
    experts, _, hidden_width = weights[0].shape
    train = weights[5].shape[2]
    groups, depth = lax.axis_size("group"), lax.axis_size("deep")
    capacity = 2 * tok // (experts * HALVES * depth)
    span = experts * depth
    rows = groups * span * capacity
    sizes = (tok, top, rows, span, capacity)
    half = lax.axis_index("half").reshape(1)
    cube = ("group", "deep")
    send_type = jax.ShapeDtypeStruct((rows, 2 * width), BF16)
    place_type = jax.ShapeDtypeStruct((tok, rows), BF16)
    pay_type = jax.ShapeDtypeStruct((tok, 2 * width + LANES), BF16)
    pay, own_send, own_place = call(
        functools.partial(own_kernel, sizes),
        (pay_type, send_type, place_type),
        [SMEM, VMEM, VMEM, VMEM, VMEM],
        (half, expert_ids.T, gate_w.T, tokens, out_grad),
    )
    swap = [(0, 1), (1, 0)]
    guest = lax.ppermute(pay, "half", swap)
    own_rows = lax.all_to_all(own_send, cube, 0, 0, tiled=True)
    guest_send, guest_place = call(
        functools.partial(guest_kernel, sizes), (send_type, place_type), [SMEM, VMEM], (half, guest)
    )
    guest_rows = lax.all_to_all(guest_send, cube, 0, 0, tiled=True)
    out_type = jax.ShapeDtypeStruct((rows, width + train), BF16)
    scratch = [pltpu.VMEM(w.shape, w.dtype) for w in weights]
    scratch += [
        pltpu.VMEM((experts, rows, weights[5].shape[1]), BF16),
        pltpu.SemaphoreType.DMA((len(weights), experts)),
    ]
    moved = sum(w.size * 2 for w in weights)
    compute = functools.partial(
        call,
        functools.partial(expert_kernel, capacity),
        out_type,
        [VMEM] + [ANY] * len(weights),
        scratch=scratch,
        flops=2 * rows * moved,
        moved=moved,
        limit=48 << 20,
    )
    own_out = compute((own_rows,) + weights)
    guest_out = compute((guest_rows,) + weights)
    guest_home = lax.all_to_all(guest_out, cube, 0, 0, tiled=True)
    part = call(
        part_kernel,
        jax.ShapeDtypeStruct((tok, width + train), BF16),
        [VMEM, VMEM],
        (guest_place, guest_home),
    )
    part = lax.ppermute(part, "half", swap)
    own_home = lax.all_to_all(own_out, cube, 0, 0, tiled=True)
    return call(
        final_kernel,
        (
            jax.ShapeDtypeStruct((tok, width), BF16),
            jax.ShapeDtypeStruct((QRY_DEV, train), F32),
        ),
        [VMEM, VMEM, VMEM, VMEM],
        (own_place, own_home, part, query_ids),
    )


def solution(mesh):
    groups, line = mesh.shape["group"], mesh.shape["expert"]
    devices = mesh.devices.reshape(groups, HALVES, line // HALVES)
    split = Mesh(devices, ("group", "half", "deep"))
    spread = ("group", "half", "deep")
    return jax.shard_map(
        body,
        mesh=split,
        in_specs=(P(spread, None),) * 5 + (P(spread, None, None),) * 6,
        out_specs=(P(spread, None), P(spread, None)),
        check_vma=False,
    )
```

```python
import functools

import jax
import jax.numpy as jnp
from jax import lax
from jax.experimental import pallas as pl
from jax.experimental.pallas import tpu as pltpu
from jax.sharding import Mesh, PartitionSpec as P


QRY_DEV = 8
PAIR = 2
LANES = 128
F32 = jnp.float32
BF16 = jnp.bfloat16
NT = (((1,), (1,)), ((), ()))
AXES = ("row", "core", "half", "deep")


def dot(a, b):
    return jnp.dot(a, b, preferred_element_type=F32)


def dot_nt(a, b):
    return lax.dot_general(a, b, NT, preferred_element_type=F32)


def pay_kernel(ids_ref, w_ref, x_ref, g_ref, pay_ref):
    top, tok = ids_ref.shape
    width = x_ref.shape[1]
    flat = jnp.concatenate([ids_ref[...].astype(F32), w_ref[...].astype(F32)], axis=0)
    flat = jnp.concatenate([flat, jnp.zeros((LANES - 2 * top, tok), F32)], axis=0)
    flat = jnp.concatenate([flat, jnp.zeros((LANES, LANES - tok), F32)], axis=1)
    pay_ref[:, :width] = x_ref[...]
    pay_ref[:, width : 2 * width] = g_ref[...]
    pay_ref[:, 2 * width :] = flat.T[:tok, :].astype(BF16)


def pack_kernel(top, experts, capacity, deep, here_ref, first_ref, second_ref, *outs):
    place_ref, sends = outs[-1], outs[:-1]
    tok = first_ref.shape[0]
    width = sends[0].shape[1] // 2
    piece = sends[0].shape[0]
    shape = (PAIR * tok, piece * len(sends))
    both = jnp.concatenate([first_ref[...], second_ref[...]], axis=0)
    meta = both[:, 2 * width :].astype(F32)
    slot = lax.broadcasted_iota(jnp.int32, shape, 1)
    block = lax.broadcasted_iota(jnp.int32, shape, 0) // tok
    chip = slot // piece
    to_row, to_deep = here_ref[0] ^ (chip // deep), here_ref[3] ^ (chip % deep)
    device = ((to_row * PAIR + here_ref[1]) * PAIR + here_ref[2]) * deep + to_deep
    expert = (device * experts + slot // (PAIR * capacity) % experts).astype(F32)
    meant = jnp.where(slot // capacity % PAIR == block, 1.0, 0.0)
    named = jnp.zeros(shape, F32)
    weight = jnp.zeros(shape, F32)
    for k in range(top):
        hit = jnp.where(meta[:, k : k + 1] == expert, meant, 0.0)
        named = named + hit
        weight = weight + hit * meta[:, top + k : top + k + 1]
    row = lax.broadcasted_iota(jnp.int32, (PAIR * tok, PAIR * tok), 0)
    col = lax.broadcasted_iota(jnp.int32, (PAIR * tok, PAIR * tok), 1)
    earlier = dot(jnp.where(col < row, 1.0, 0.0).astype(BF16), named.astype(BF16))
    place = jnp.where(earlier == (slot % capacity).astype(F32), named, 0.0)
    place_ref[...] = place.astype(BF16)
    pick = place.T.astype(BF16)
    scale = jnp.sum((place * weight).T, axis=1, keepdims=True)
    x = dot(pick, both[:, :width]).astype(BF16)
    delta = (scale * dot(pick, both[:, width : 2 * width])).astype(BF16)
    for i, send in enumerate(sends):
        send[:, :width] = x[i * piece : (i + 1) * piece]
        send[:, width:] = delta[i * piece : (i + 1) * piece]


def expert_kernel(count, group, *refs):
    ins, hbm, outs, vmem = (
        refs[:count],
        refs[count : count + 6],
        refs[count + 6 : 2 * count + 6],
        refs[2 * count + 6 : 2 * count + 12],
    )
    outer_ref, sem = refs[2 * count + 12 :]
    gate, up, down, left_proj, right_proj, stored = vmem
    experts, width, _ = gate.shape
    rank = left_proj.shape[1]
    piece = ins[0].shape[0]
    rows = piece * count

    def copy(i, j):
        return pltpu.make_async_copy(hbm[i].at[j], vmem[i].at[j], sem.at[i, j])

    for j in range(experts):
        for i in range(5):
            copy(i, j).start()
    for j in range(experts):
        copy(5, j).start()
    x = jnp.concatenate([r[:, :width] for r in ins], axis=0)
    delta = jnp.concatenate([r[:, width:] for r in ins], axis=0)
    owner = lax.broadcasted_iota(jnp.int32, (rows, 1), 0) // group % experts
    left = jnp.zeros((rows, rank), F32)
    right = jnp.zeros((rows, rank), F32)
    grad = jnp.zeros((rows, width), F32)
    for j in range(experts):
        mine = owner == j
        copy(0, j).wait()
        a_gate = dot(x, gate[j])
        copy(1, j).wait()
        a_up = dot(x, up[j])
        copy(2, j).wait()
        d_hidden = dot_nt(delta, down[j])
        sig = jax.nn.sigmoid(a_gate)
        active = a_gate * sig
        hidden = (active * a_up).astype(BF16)
        grad_up = jnp.where(mine, d_hidden * active, 0.0).astype(BF16)
        grad_gate = jnp.where(
            mine, d_hidden * a_up * sig * (1.0 + a_gate * (1.0 - sig)), 0.0
        ).astype(BF16)
        grad = grad + dot_nt(grad_gate, gate[j])
        grad = grad + dot_nt(grad_up, up[j])
        copy(3, j).wait()
        left = jnp.where(mine, dot_nt(delta, left_proj[j]), left)
        copy(4, j).wait()
        right = jnp.where(mine, dot_nt(hidden, right_proj[j]), right)
    grad = grad.astype(BF16)
    per = LANES // rank
    wide = jnp.concatenate([right] * per, axis=1)
    lane = lax.broadcasted_iota(jnp.int32, (rows, LANES), 1) // rank
    for c in range(rank // per):
        factor = left[:, c * per : c * per + 1]
        for k in range(1, per):
            factor = jnp.where(lane == k, left[:, c * per + k : c * per + k + 1], factor)
        outer = factor * wide
        for j in range(experts):
            outer_ref[j, :, c * LANES : (c + 1) * LANES] = jnp.where(owner == j, outer, 0.0).astype(
                BF16
            )
    score = jnp.zeros((rows, stored.shape[2]), F32)
    for j in range(experts):
        copy(5, j).wait()
        score = score + dot(outer_ref[j], stored[j])
    score = score.astype(BF16)
    for i, out in enumerate(outs):
        out[:, :width] = grad[i * piece : (i + 1) * piece]
        out[:, width:] = score[i * piece : (i + 1) * piece]


def part_kernel(place_ref, *refs):
    ins, keep_ref, give_ref = refs[:-2], refs[-2], refs[-1]
    tok = keep_ref.shape[0]
    total = dot(place_ref[...], jnp.concatenate([r[...] for r in ins], axis=0))
    keep_ref[...] = total[:tok]
    give_ref[...] = total[tok:].astype(BF16)


def join_kernel(keep_ref, more_ref, out_ref):
    out_ref[...] = (keep_ref[...] + more_ref[...].astype(F32)).astype(BF16)


def final_kernel(keep_ref, more_ref, far_ref, query_ref, grad_ref, score_ref):
    width = grad_ref.shape[1]
    total = keep_ref[...] + more_ref[...].astype(F32) + far_ref[...].astype(F32)
    grad_ref[...] = total[:, :width].astype(BF16)
    wanted = lax.broadcasted_iota(jnp.int32, (score_ref.shape[0], query_ref.shape[1]), 0)
    pick = jnp.where(query_ref[...] == wanted, 1.0, 0.0)
    score_ref[...] = jnp.dot(
        pick, total[:, width:], precision=lax.Precision.HIGHEST, preferred_element_type=F32
    )


VMEM = pl.BlockSpec(memory_space=pltpu.VMEM)
SMEM = pl.BlockSpec(memory_space=pltpu.SMEM)
HBM = pl.BlockSpec(memory_space=pltpu.HBM)


def call(kernel, outs, in_specs, args, scratch=(), flops=1_000_000, moved=1_000_000, limit=8 << 20):
    return pl.pallas_call(
        kernel,
        out_shape=outs,
        in_specs=in_specs,
        out_specs=jax.tree.map(lambda _: VMEM, outs),
        scratch_shapes=scratch,
        compiler_params=pltpu.CompilerParams(vmem_limit_bytes=limit),
        cost_estimate=pl.CostEstimate(flops=flops, bytes_accessed=moved, transcendentals=0),
    )(*args)


def layer(tokens, out_grad, expert_ids, gate_w, query_ids, *weights):
    weights = weights[:3] + tuple(w.transpose(0, 2, 1) for w in weights[3:5]) + weights[5:]
    tok, width = tokens.shape
    top = expert_ids.shape[1]
    experts = weights[0].shape[0]
    train = weights[5].shape[2]
    row_size, deep = lax.axis_size("row"), lax.axis_size("deep")
    chips = row_size * deep
    capacity = 2 * tok // (experts * PAIR * deep)
    piece = experts * PAIR * capacity
    here = jnp.stack([lax.axis_index(a) for a in AXES]).astype(jnp.int32)
    shape = jax.ShapeDtypeStruct

    def swap(value, row=0, core=0, half=0, far=0):
        pairs = []
        for r in range(row_size):
            for c in range(PAIR):
                for h in range(PAIR):
                    for d in range(deep):
                        source = ((r * PAIR + c) * PAIR + h) * deep + d
                        target = (((r ^ row) * PAIR + (c ^ core)) * PAIR + (h ^ half)) * deep
                        pairs.append((source, target + (d ^ far)))
        return lax.ppermute(value, AXES, pairs)

    def exchange(pieces):
        order = sorted(range(1, chips), key=lambda o: -bin(o).count("1"))
        moved = {o: swap(pieces[o], row=o // deep, far=o % deep) for o in order}
        return [pieces[0]] + [moved[o] for o in range(1, chips)]

    def pack(first, second):
        outs = (shape((piece, 2 * width), BF16),) * chips
        outs += (shape((PAIR * tok, piece * chips), BF16),)
        kernel = functools.partial(pack_kernel, top, experts, capacity, deep)
        filled = call(kernel, outs, [SMEM, VMEM, VMEM], (here, first, second), limit=12 << 20)
        return filled[:-1], filled[-1]

    def part(place, pieces):
        outs = (shape((tok, width + train), F32), shape((tok, width + train), BF16))
        return call(part_kernel, outs, [VMEM] * (1 + chips), (place, *pieces))

    pay = call(
        pay_kernel,
        shape((tok, 2 * width + LANES), BF16),
        [VMEM] * 4,
        (expert_ids.T, gate_w.T, tokens, out_grad),
    )
    guest = swap(pay, half=1)
    other = swap(pay, core=1)
    own_send, own_place = pack(pay, other)
    own_rows = exchange(own_send)
    other = swap(guest, core=1)
    guest_send, guest_place = pack(guest, other)
    guest_rows = exchange(guest_send)
    rows = 2 * chips * piece
    size = sum(w.size for w in weights)
    outs = call(
        functools.partial(expert_kernel, 2 * chips, PAIR * capacity),
        (shape((piece, width + train), BF16),) * (2 * chips),
        [VMEM] * (2 * chips) + [HBM] * len(weights),
        (*own_rows, *guest_rows, *weights),
        scratch=[pltpu.VMEM(w.shape, w.dtype) for w in weights]
        + [
            pltpu.VMEM((experts, rows, weights[5].shape[1]), BF16),
            pltpu.SemaphoreType.DMA((len(weights), experts)),
        ],
        flops=2 * rows * size,
        moved=2 * size,
        limit=50 << 20,
    )
    guest_back = exchange(outs[chips:])
    own_back = exchange(outs[:chips])
    guest_keep, guest_give = part(guest_place, guest_back)
    more = swap(guest_give, core=1)
    far = call(join_kernel, shape((tok, width + train), BF16), [VMEM] * 2, (guest_keep, more))
    far = swap(far, half=1)
    own_keep, own_give = part(own_place, own_back)
    more = swap(own_give, core=1)
    return call(
        final_kernel,
        (shape((tok, width), BF16), shape((QRY_DEV, train), F32)),
        [VMEM] * 4,
        (own_keep, more, far, query_ids),
    )


def solution(mesh):
    groups, line = mesh.shape["group"], mesh.shape["expert"]
    devices = mesh.devices.reshape(groups // PAIR, PAIR, PAIR, line // PAIR)
    return jax.shard_map(
        layer,
        mesh=Mesh(devices, AXES),
        in_specs=(P(AXES, None),) * 5 + (P(AXES, None, None),) * 6,
        out_specs=(P(AXES, None), P(AXES, None)),
        check_vma=False,
    )
```

```python
import functools

import jax
import jax.numpy as jnp
from jax import lax
from jax.experimental import pallas as pl
from jax.experimental.pallas import tpu as pltpu
from jax.sharding import Mesh, PartitionSpec as P


QRY_DEV = 8
PAIR = 2
LANES = 128
F32 = jnp.float32
BF16 = jnp.bfloat16
NT = (((1,), (1,)), ((), ()))
AXES = ("row", "core", "half", "deep")


def dot(a, b):
    return jnp.dot(a, b, preferred_element_type=F32)


def dot_nt(a, b):
    return lax.dot_general(a, b, NT, preferred_element_type=F32)


def pay_kernel(ids_hbm, w_hbm, x_hbm, g_hbm, pay_ref, ids_ref, w_ref, x_ref, g_ref, sem):
    top, tok = ids_ref.shape
    width = x_ref.shape[1]
    pairs = ((ids_hbm, ids_ref), (w_hbm, w_ref), (x_hbm, x_ref), (g_hbm, g_ref))
    copies = [pltpu.make_async_copy(a, b, sem.at[i]) for i, (a, b) in enumerate(pairs)]
    for copy in copies:
        copy.start()
    copies[0].wait()
    copies[1].wait()
    flat = jnp.concatenate([ids_ref[...].astype(F32), w_ref[...].astype(F32)], axis=0)
    flat = jnp.concatenate([flat, jnp.zeros((LANES - 2 * top, tok), F32)], axis=0)
    flat = jnp.concatenate([flat, jnp.zeros((LANES, LANES - tok), F32)], axis=1)
    pay_ref[:, 2 * width :] = flat.T[:tok, :].astype(BF16)
    copies[2].wait()
    pay_ref[:, :width] = x_ref[...]
    copies[3].wait()
    pay_ref[:, width : 2 * width] = g_ref[...]


def pack_kernel(top, experts, capacity, deep, here_ref, first_ref, second_ref, *outs):
    place_ref, sends = outs[-1], outs[:-1]
    tok = first_ref.shape[0]
    width = sends[0].shape[1] // 2
    piece = sends[0].shape[0]
    shape = (PAIR * tok, piece * len(sends))
    both = jnp.concatenate([first_ref[...], second_ref[...]], axis=0)
    meta = both[:, 2 * width :].astype(F32)
    slot = lax.broadcasted_iota(jnp.int32, shape, 1)
    block = lax.broadcasted_iota(jnp.int32, shape, 0) // tok
    chip = slot // piece
    to_row, to_deep = here_ref[0] ^ (chip // deep), here_ref[3] ^ (chip % deep)
    device = ((to_row * PAIR + here_ref[1]) * PAIR + here_ref[2]) * deep + to_deep
    expert = (device * experts + slot // (PAIR * capacity) % experts).astype(F32)
    meant = jnp.where(slot // capacity % PAIR == block, 1.0, 0.0)
    named = jnp.zeros(shape, F32)
    weight = jnp.zeros(shape, F32)
    for k in range(top):
        hit = jnp.where(meta[:, k : k + 1] == expert, meant, 0.0)
        named = named + hit
        weight = weight + hit * meta[:, top + k : top + k + 1]
    row = lax.broadcasted_iota(jnp.int32, (PAIR * tok, PAIR * tok), 0)
    col = lax.broadcasted_iota(jnp.int32, (PAIR * tok, PAIR * tok), 1)
    earlier = dot(jnp.where(col < row, 1.0, 0.0).astype(BF16), named.astype(BF16))
    place = jnp.where(earlier == (slot % capacity).astype(F32), named, 0.0)
    place_ref[...] = place.astype(BF16)
    pick = place.T.astype(BF16)
    scale = jnp.sum((place * weight).T, axis=1, keepdims=True)
    x = dot(pick, both[:, :width]).astype(BF16)
    delta = (scale * dot(pick, both[:, width : 2 * width])).astype(BF16)
    for i, send in enumerate(sends):
        send[:, :width] = x[i * piece : (i + 1) * piece]
        send[:, width:] = delta[i * piece : (i + 1) * piece]


def expert_kernel(count, group, *refs):
    ins, hbm, outs, vmem = (
        refs[:count],
        refs[count : count + 6],
        refs[count + 6 : 2 * count + 6],
        refs[2 * count + 6 : 2 * count + 12],
    )
    outer_ref, sem = refs[2 * count + 12 :]
    gate, up, down, left_proj, right_proj, stored = vmem
    experts, width, _ = gate.shape
    rank = left_proj.shape[1]
    piece = ins[0].shape[0]
    rows = piece * count

    def copy(i, j):
        return pltpu.make_async_copy(hbm[i].at[j], vmem[i].at[j], sem.at[i, j])

    for j in range(experts):
        for i in range(5):
            copy(i, j).start()
    for j in range(experts):
        copy(5, j).start()
    x = jnp.concatenate([r[:, :width] for r in ins], axis=0)
    delta = jnp.concatenate([r[:, width:] for r in ins], axis=0)
    owner = lax.broadcasted_iota(jnp.int32, (rows, 1), 0) // group % experts
    left = jnp.zeros((rows, rank), F32)
    right = jnp.zeros((rows, rank), F32)
    grad = jnp.zeros((rows, width), F32)
    for j in range(experts):
        mine = owner == j
        copy(0, j).wait()
        a_gate = dot(x, gate[j])
        copy(1, j).wait()
        a_up = dot(x, up[j])
        copy(2, j).wait()
        d_hidden = dot_nt(delta, down[j])
        sig = jax.nn.sigmoid(a_gate)
        active = a_gate * sig
        hidden = (active * a_up).astype(BF16)
        grad_up = jnp.where(mine, d_hidden * active, 0.0).astype(BF16)
        grad_gate = jnp.where(
            mine, d_hidden * a_up * sig * (1.0 + a_gate * (1.0 - sig)), 0.0
        ).astype(BF16)
        grad = grad + dot_nt(grad_gate, gate[j])
        grad = grad + dot_nt(grad_up, up[j])
        copy(3, j).wait()
        left = jnp.where(mine, dot_nt(delta, left_proj[j]), left)
        copy(4, j).wait()
        right = jnp.where(mine, dot_nt(hidden, right_proj[j]), right)
    grad = grad.astype(BF16)
    per = LANES // rank
    wide = jnp.concatenate([right] * per, axis=1)
    lane = lax.broadcasted_iota(jnp.int32, (rows, LANES), 1) // rank
    for c in range(rank // per):
        factor = left[:, c * per : c * per + 1]
        for k in range(1, per):
            factor = jnp.where(lane == k, left[:, c * per + k : c * per + k + 1], factor)
        outer = factor * wide
        for j in range(experts):
            outer_ref[j, :, c * LANES : (c + 1) * LANES] = jnp.where(owner == j, outer, 0.0).astype(
                BF16
            )
    score = jnp.zeros((rows, stored.shape[2]), F32)
    for j in range(experts):
        copy(5, j).wait()
        score = score + dot(outer_ref[j], stored[j])
    score = score.astype(BF16)
    for i, out in enumerate(outs):
        out[:, :width] = grad[i * piece : (i + 1) * piece]
        out[:, width:] = score[i * piece : (i + 1) * piece]


def part_kernel(place_ref, *refs):
    ins, keep_ref, give_ref = refs[:-2], refs[-2], refs[-1]
    tok = keep_ref.shape[0]
    total = dot(place_ref[...], jnp.concatenate([r[...] for r in ins], axis=0))
    keep_ref[...] = total[:tok]
    give_ref[...] = total[tok:].astype(BF16)


def join_kernel(keep_ref, more_ref, out_ref):
    out_ref[...] = (keep_ref[...] + more_ref[...].astype(F32)).astype(BF16)


def final_kernel(keep_ref, more_ref, far_ref, query_ref, grad_ref, score_ref):
    width = grad_ref.shape[1]
    total = keep_ref[...] + more_ref[...].astype(F32) + far_ref[...].astype(F32)
    grad_ref[...] = total[:, :width].astype(BF16)
    wanted = lax.broadcasted_iota(jnp.int32, (score_ref.shape[0], query_ref.shape[1]), 0)
    pick = jnp.where(query_ref[...] == wanted, 1.0, 0.0)
    score_ref[...] = jnp.dot(
        pick, total[:, width:], precision=lax.Precision.HIGHEST, preferred_element_type=F32
    )


VMEM = pl.BlockSpec(memory_space=pltpu.VMEM)
SMEM = pl.BlockSpec(memory_space=pltpu.SMEM)
HBM = pl.BlockSpec(memory_space=pltpu.HBM)


def in_hbm(value):
    return pltpu.with_memory_space_constraint(value, pltpu.HBM)


def call(kernel, outs, in_specs, args, scratch=(), flops=1_000_000, moved=1_000_000, limit=8 << 20):
    return pl.pallas_call(
        kernel,
        out_shape=outs,
        in_specs=in_specs,
        out_specs=jax.tree.map(lambda _: VMEM, outs),
        scratch_shapes=scratch,
        compiler_params=pltpu.CompilerParams(vmem_limit_bytes=limit),
        cost_estimate=pl.CostEstimate(flops=flops, bytes_accessed=moved, transcendentals=0),
    )(*args)


def layer(tokens, out_grad, expert_ids, gate_w, query_ids, *weights):
    weights = weights[:3] + tuple(w.transpose(0, 2, 1) for w in weights[3:5]) + weights[5:]
    weights = tuple(in_hbm(w) for w in weights)
    tok, width = tokens.shape
    top = expert_ids.shape[1]
    experts = weights[0].shape[0]
    train = weights[5].shape[2]
    row_size, deep = lax.axis_size("row"), lax.axis_size("deep")
    chips = row_size * deep
    capacity = 2 * tok // (experts * PAIR * deep)
    piece = experts * PAIR * capacity
    here = jnp.stack([lax.axis_index(a) for a in AXES]).astype(jnp.int32)
    shape = jax.ShapeDtypeStruct

    def swap(value, row=0, core=0, half=0, far=0):
        pairs = []
        for r in range(row_size):
            for c in range(PAIR):
                for h in range(PAIR):
                    for d in range(deep):
                        source = ((r * PAIR + c) * PAIR + h) * deep + d
                        target = (((r ^ row) * PAIR + (c ^ core)) * PAIR + (h ^ half)) * deep
                        pairs.append((source, target + (d ^ far)))
        return lax.ppermute(value, AXES, pairs)

    def exchange(pieces):
        order = sorted(range(1, chips), key=lambda o: -bin(o).count("1"))
        moved = {o: swap(pieces[o], row=o // deep, far=o % deep) for o in order}
        return [pieces[0]] + [moved[o] for o in range(1, chips)]

    def pack(first, second):
        outs = (shape((piece, 2 * width), BF16),) * chips
        outs += (shape((PAIR * tok, piece * chips), BF16),)
        kernel = functools.partial(pack_kernel, top, experts, capacity, deep)
        filled = call(kernel, outs, [SMEM, VMEM, VMEM], (here, first, second), limit=12 << 20)
        return filled[:-1], filled[-1]

    def part(place, pieces):
        outs = (shape((tok, width + train), F32), shape((tok, width + train), BF16))
        return call(part_kernel, outs, [VMEM] * (1 + chips), (place, *pieces))

    inputs = tuple(in_hbm(v) for v in (expert_ids.T, gate_w.T, tokens, out_grad))
    pay = call(
        pay_kernel,
        shape((tok, 2 * width + LANES), BF16),
        [HBM] * 4,
        inputs,
        scratch=[pltpu.VMEM(v.shape, v.dtype) for v in inputs]
        + [pltpu.SemaphoreType.DMA((len(inputs),))],
    )
    guest = swap(pay, half=1)
    other = swap(pay, core=1)
    own_send, own_place = pack(pay, other)
    own_rows = exchange(own_send)
    other = swap(guest, core=1)
    guest_send, guest_place = pack(guest, other)
    guest_rows = exchange(guest_send)
    rows = 2 * chips * piece
    size = sum(w.size for w in weights)
    outs = call(
        functools.partial(expert_kernel, 2 * chips, PAIR * capacity),
        (shape((piece, width + train), BF16),) * (2 * chips),
        [VMEM] * (2 * chips) + [HBM] * len(weights),
        (*own_rows, *guest_rows, *weights),
        scratch=[pltpu.VMEM(w.shape, w.dtype) for w in weights]
        + [
            pltpu.VMEM((experts, rows, weights[5].shape[1]), BF16),
            pltpu.SemaphoreType.DMA((len(weights), experts)),
        ],
        flops=2 * rows * size,
        moved=2 * size,
        limit=50 << 20,
    )
    guest_back = exchange(outs[chips:])
    own_back = exchange(outs[:chips])
    guest_keep, guest_give = part(guest_place, guest_back)
    more = swap(guest_give, core=1)
    far = call(join_kernel, shape((tok, width + train), BF16), [VMEM] * 2, (guest_keep, more))
    far = swap(far, half=1)
    own_keep, own_give = part(own_place, own_back)
    more = swap(own_give, core=1)
    return call(
        final_kernel,
        (shape((tok, width), BF16), shape((QRY_DEV, train), F32)),
        [VMEM] * 4,
        (own_keep, more, far, query_ids),
    )


def solution(mesh):
    groups, line = mesh.shape["group"], mesh.shape["expert"]
    devices = mesh.devices.reshape(groups // PAIR, PAIR, PAIR, line // PAIR)
    return jax.shard_map(
        layer,
        mesh=Mesh(devices, AXES),
        in_specs=(P(AXES, None),) * 5 + (P(AXES, None, None),) * 6,
        out_specs=(P(AXES, None), P(AXES, None)),
        check_vma=False,
    )
```

```python
import functools

import jax
import jax.numpy as jnp
from jax import lax
from jax.experimental import pallas as pl
from jax.experimental.pallas import tpu as pltpu
from jax.sharding import Mesh, PartitionSpec as P


QRY_DEV = 8
PAIR = 2
LANES = 128
F32 = jnp.float32
BF16 = jnp.bfloat16
NT = (((1,), (1,)), ((), ()))
AXES = ("row", "core", "half", "deep")


def dot(a, b):
    return jnp.dot(a, b, preferred_element_type=F32)


def dot_nt(a, b):
    return lax.dot_general(a, b, NT, preferred_element_type=F32)


def pay_kernel(ids_hbm, w_hbm, x_hbm, g_hbm, pay_ref, ids_ref, w_ref, x_ref, g_ref, sem):
    top, tok = ids_ref.shape
    width = x_ref.shape[1]
    pairs = ((ids_hbm, ids_ref), (w_hbm, w_ref), (x_hbm, x_ref), (g_hbm, g_ref))
    copies = [pltpu.make_async_copy(a, b, sem.at[i]) for i, (a, b) in enumerate(pairs)]
    for copy in copies:
        copy.start()
    copies[0].wait()
    copies[1].wait()
    flat = jnp.concatenate([ids_ref[...].astype(F32), w_ref[...].astype(F32)], axis=0)
    flat = jnp.concatenate([flat, jnp.zeros((LANES - 2 * top, tok), F32)], axis=0)
    flat = jnp.concatenate([flat, jnp.zeros((LANES, LANES - tok), F32)], axis=1)
    pay_ref[:, 2 * width :] = flat.T[:tok, :].astype(BF16)
    copies[2].wait()
    pay_ref[:, :width] = x_ref[...]
    copies[3].wait()
    pay_ref[:, width : 2 * width] = g_ref[...]


def pack_kernel(top, experts, capacity, deep, here_ref, first_ref, second_ref, *outs):
    place_ref, sends = outs[-1], outs[:-1]
    tok = first_ref.shape[0]
    width = sends[0].shape[1] // 2
    piece = sends[0].shape[0]
    shape = (PAIR * tok, piece * len(sends))
    both = jnp.concatenate([first_ref[...], second_ref[...]], axis=0)
    meta = both[:, 2 * width :].astype(F32)
    slot = lax.broadcasted_iota(jnp.int32, shape, 1)
    block = lax.broadcasted_iota(jnp.int32, shape, 0) // tok
    chip = slot // piece
    to_row, to_deep = here_ref[0] ^ (chip // deep), here_ref[3] ^ (chip % deep)
    device = ((to_row * PAIR + here_ref[1]) * PAIR + here_ref[2]) * deep + to_deep
    expert = (device * experts + slot // (PAIR * capacity) % experts).astype(F32)
    meant = jnp.where(slot // capacity % PAIR == block, 1.0, 0.0)
    named = jnp.zeros(shape, F32)
    weight = jnp.zeros(shape, F32)
    for k in range(top):
        hit = jnp.where(meta[:, k : k + 1] == expert, meant, 0.0)
        named = named + hit
        weight = weight + hit * meta[:, top + k : top + k + 1]
    row = lax.broadcasted_iota(jnp.int32, (PAIR * tok, PAIR * tok), 0)
    col = lax.broadcasted_iota(jnp.int32, (PAIR * tok, PAIR * tok), 1)
    earlier = dot(jnp.where(col < row, 1.0, 0.0).astype(BF16), named.astype(BF16))
    place = jnp.where(earlier == (slot % capacity).astype(F32), named, 0.0)
    place_ref[...] = place.astype(BF16)
    pick = place.T.astype(BF16)
    scale = jnp.sum((place * weight).T, axis=1, keepdims=True)
    x = dot(pick, both[:, :width]).astype(BF16)
    delta = (scale * dot(pick, both[:, width : 2 * width])).astype(BF16)
    for i, send in enumerate(sends):
        send[:, :width] = x[i * piece : (i + 1) * piece]
        send[:, width:] = delta[i * piece : (i + 1) * piece]


def load_kernel(*refs):
    count = len(refs) // 2
    sem = refs[-1]
    copies = [pltpu.make_async_copy(refs[i], refs[count + i], sem.at[i]) for i in range(count)]
    for copy in copies:
        copy.start()
    for copy in copies:
        copy.wait()


def expert_kernel(count, group, *refs):
    ins, weights, outs = refs[:count], refs[count : count + 6], refs[count + 6 : 2 * count + 6]
    gate, up, down, left_proj, right_proj, stored = weights
    outer_ref = refs[-1]
    experts, width, _ = gate.shape
    rank = left_proj.shape[1]
    piece = ins[0].shape[0]
    rows = piece * count
    x = jnp.concatenate([r[:, :width] for r in ins], axis=0)
    delta = jnp.concatenate([r[:, width:] for r in ins], axis=0)
    owner = lax.broadcasted_iota(jnp.int32, (rows, 1), 0) // group % experts
    left = jnp.zeros((rows, rank), F32)
    right = jnp.zeros((rows, rank), F32)
    grad = jnp.zeros((rows, width), F32)
    for j in range(experts):
        mine = owner == j
        a_gate = dot(x, gate[j])
        a_up = dot(x, up[j])
        d_hidden = dot_nt(delta, down[j])
        sig = jax.nn.sigmoid(a_gate)
        active = a_gate * sig
        hidden = (active * a_up).astype(BF16)
        grad_up = jnp.where(mine, d_hidden * active, 0.0).astype(BF16)
        grad_gate = jnp.where(
            mine, d_hidden * a_up * sig * (1.0 + a_gate * (1.0 - sig)), 0.0
        ).astype(BF16)
        grad = grad + dot_nt(grad_gate, gate[j])
        grad = grad + dot_nt(grad_up, up[j])
        left = jnp.where(mine, dot_nt(delta, left_proj[j]), left)
        right = jnp.where(mine, dot_nt(hidden, right_proj[j]), right)
    grad = grad.astype(BF16)
    per = LANES // rank
    wide = jnp.concatenate([right] * per, axis=1)
    lane = lax.broadcasted_iota(jnp.int32, (rows, LANES), 1) // rank
    for c in range(rank // per):
        factor = left[:, c * per : c * per + 1]
        for k in range(1, per):
            factor = jnp.where(lane == k, left[:, c * per + k : c * per + k + 1], factor)
        outer = factor * wide
        for j in range(experts):
            outer_ref[j, :, c * LANES : (c + 1) * LANES] = jnp.where(owner == j, outer, 0.0).astype(
                BF16
            )
    score = jnp.zeros((rows, stored.shape[2]), F32)
    for j in range(experts):
        score = score + dot(outer_ref[j], stored[j])
    score = score.astype(BF16)
    for i, out in enumerate(outs):
        out[:, :width] = grad[i * piece : (i + 1) * piece]
        out[:, width:] = score[i * piece : (i + 1) * piece]


def part_kernel(place_ref, *refs):
    ins, keep_ref, give_ref = refs[:-2], refs[-2], refs[-1]
    tok = keep_ref.shape[0]
    total = dot(place_ref[...], jnp.concatenate([r[...] for r in ins], axis=0))
    keep_ref[...] = total[:tok]
    give_ref[...] = total[tok:].astype(BF16)


def join_kernel(keep_ref, more_ref, out_ref):
    out_ref[...] = (keep_ref[...] + more_ref[...].astype(F32)).astype(BF16)


def final_kernel(keep_ref, more_ref, far_ref, query_ref, grad_ref, score_ref):
    width = grad_ref.shape[1]
    total = keep_ref[...] + more_ref[...].astype(F32) + far_ref[...].astype(F32)
    grad_ref[...] = total[:, :width].astype(BF16)
    wanted = lax.broadcasted_iota(jnp.int32, (score_ref.shape[0], query_ref.shape[1]), 0)
    pick = jnp.where(query_ref[...] == wanted, 1.0, 0.0)
    score_ref[...] = jnp.dot(
        pick, total[:, width:], precision=lax.Precision.HIGHEST, preferred_element_type=F32
    )


VMEM = pl.BlockSpec(memory_space=pltpu.VMEM)
SMEM = pl.BlockSpec(memory_space=pltpu.SMEM)
HBM = pl.BlockSpec(memory_space=pltpu.HBM)


def in_hbm(value):
    return pltpu.with_memory_space_constraint(value, pltpu.HBM)


def call(kernel, outs, in_specs, args, scratch=(), flops=1_000_000, moved=1_000_000, limit=8 << 20):
    return pl.pallas_call(
        kernel,
        out_shape=outs,
        in_specs=in_specs,
        out_specs=jax.tree.map(lambda _: VMEM, outs),
        scratch_shapes=scratch,
        compiler_params=pltpu.CompilerParams(vmem_limit_bytes=limit),
        cost_estimate=pl.CostEstimate(flops=flops, bytes_accessed=moved, transcendentals=0),
    )(*args)


def layer(tokens, out_grad, expert_ids, gate_w, query_ids, *weights):
    weights = weights[:3] + tuple(w.transpose(0, 2, 1) for w in weights[3:5]) + weights[5:]
    weights = tuple(in_hbm(w) for w in weights)
    tok, width = tokens.shape
    top = expert_ids.shape[1]
    experts = weights[0].shape[0]
    train = weights[5].shape[2]
    row_size, deep = lax.axis_size("row"), lax.axis_size("deep")
    chips = row_size * deep
    capacity = 2 * tok // (experts * PAIR * deep)
    piece = experts * PAIR * capacity
    here = jnp.stack([lax.axis_index(a) for a in AXES]).astype(jnp.int32)
    shape = jax.ShapeDtypeStruct

    def swap(value, row=0, core=0, half=0, far=0):
        pairs = []
        for r in range(row_size):
            for c in range(PAIR):
                for h in range(PAIR):
                    for d in range(deep):
                        source = ((r * PAIR + c) * PAIR + h) * deep + d
                        target = (((r ^ row) * PAIR + (c ^ core)) * PAIR + (h ^ half)) * deep
                        pairs.append((source, target + (d ^ far)))
        return lax.ppermute(value, AXES, pairs)

    order = sorted(range(1, chips), key=lambda o: (-bin(o).count("1"), -o))

    def move(pieces, offsets):
        return {o: swap(pieces[o], row=o // deep, far=o % deep) for o in offsets}

    def exchange(pieces):
        moved = move(pieces, order)
        return [pieces[0]] + [moved[o] for o in range(1, chips)]

    def pack(first, second):
        outs = (shape((piece, 2 * width), BF16),) * chips
        outs += (shape((PAIR * tok, piece * chips), BF16),)
        kernel = functools.partial(pack_kernel, top, experts, capacity, deep)
        filled = call(kernel, outs, [SMEM, VMEM, VMEM], (here, first, second), limit=12 << 20)
        return filled[:-1], filled[-1]

    def part(place, pieces):
        outs = (shape((tok, width + train), F32), shape((tok, width + train), BF16))
        return call(part_kernel, outs, [VMEM] * (1 + chips), (place, *pieces))

    inputs = tuple(in_hbm(v) for v in (expert_ids.T, gate_w.T, tokens, out_grad))
    pay = call(
        pay_kernel,
        shape((tok, 2 * width + LANES), BF16),
        [HBM] * 4,
        inputs,
        scratch=[pltpu.VMEM(v.shape, v.dtype) for v in inputs]
        + [pltpu.SemaphoreType.DMA((len(inputs),))],
    )
    guest = swap(pay, half=1)
    other = swap(pay, core=1)
    own_send, own_place = pack(pay, other)
    own_rows = exchange(own_send)
    other = swap(guest, core=1)
    guest_send, guest_place = pack(guest, other)
    guest_rows = exchange(guest_send)
    held = pl.pallas_call(
        load_kernel,
        out_shape=tuple(pltpu.VMEM(w.shape, w.dtype) for w in weights),
        in_specs=[HBM] * len(weights),
        out_specs=(VMEM,) * len(weights),
        scratch_shapes=[pltpu.SemaphoreType.DMA((len(weights),))],
        compiler_params=pltpu.CompilerParams(vmem_limit_bytes=1 << 20),
    )(*weights)
    rows = 2 * chips * piece
    size = sum(w.size for w in weights)
    outs = call(
        functools.partial(expert_kernel, 2 * chips, PAIR * capacity),
        (shape((piece, width + train), BF16),) * (2 * chips),
        [VMEM] * (2 * chips + len(weights)),
        (*own_rows, *guest_rows, *held),
        scratch=[pltpu.VMEM((experts, rows, weights[5].shape[1]), BF16)],
        flops=2 * rows * size,
        moved=2 * size,
        limit=rows * (76 << 10),
    )
    guest_back = exchange(outs[chips:])
    early = (chips - 1) // 2
    moved = move(outs[:chips], order[:early])
    moved.update(move(outs[:chips], order[early:]))
    own_back = [outs[0]] + [moved[o] for o in range(1, chips)]
    guest_keep, guest_give = part(guest_place, guest_back)
    more = swap(guest_give, core=1)
    far = call(join_kernel, shape((tok, width + train), BF16), [VMEM] * 2, (guest_keep, more))
    far = swap(far, half=1)
    own_keep, own_give = part(own_place, own_back)
    more = swap(own_give, core=1)
    return call(
        final_kernel,
        (shape((tok, width), BF16), shape((QRY_DEV, train), F32)),
        [VMEM] * 4,
        (own_keep, more, far, query_ids),
    )


def solution(mesh):
    groups, line = mesh.shape["group"], mesh.shape["expert"]
    devices = mesh.devices.reshape(groups // PAIR, PAIR, PAIR, line // PAIR)
    return jax.shard_map(
        layer,
        mesh=Mesh(devices, AXES),
        in_specs=(P(AXES, None),) * 5 + (P(AXES, None, None),) * 6,
        out_specs=(P(AXES, None), P(AXES, None)),
        check_vma=False,
    )
```

```python
import functools

import jax
import jax.numpy as jnp
from jax import lax
from jax.experimental import pallas as pl
from jax.experimental.pallas import tpu as pltpu
from jax.sharding import Mesh, PartitionSpec as P


QRY_DEV = 8
PAIR = 2
LANES = 128
F32 = jnp.float32
BF16 = jnp.bfloat16
NT = (((1,), (1,)), ((), ()))
AXES = ("row", "core", "half", "deep")


def dot(a, b):
    return jnp.dot(a, b, preferred_element_type=F32)


def dot_nt(a, b):
    return lax.dot_general(a, b, NT, preferred_element_type=F32)


def pay_kernel(ids_hbm, w_hbm, x_hbm, g_hbm, pay_ref, ids_ref, w_ref, x_ref, g_ref, sem):
    top, tok = ids_ref.shape
    width = x_ref.shape[1]
    pairs = ((ids_hbm, ids_ref), (w_hbm, w_ref), (x_hbm, x_ref), (g_hbm, g_ref))
    copies = [pltpu.make_async_copy(a, b, sem.at[i]) for i, (a, b) in enumerate(pairs)]
    for copy in copies:
        copy.start()
    copies[0].wait()
    copies[1].wait()
    flat = jnp.concatenate([ids_ref[...].astype(F32), w_ref[...].astype(F32)], axis=0)
    flat = jnp.concatenate([flat, jnp.zeros((LANES - 2 * top, tok), F32)], axis=0)
    flat = jnp.concatenate([flat, jnp.zeros((LANES, LANES - tok), F32)], axis=1)
    pay_ref[:, 2 * width :] = flat.T[:tok, :].astype(BF16)
    copies[2].wait()
    pay_ref[:, :width] = x_ref[...]
    copies[3].wait()
    pay_ref[:, width : 2 * width] = g_ref[...]


def pack_kernel(top, experts, capacity, deep, here_ref, first_ref, second_ref, *outs):
    place_ref, sends = outs[-1], outs[:-1]
    tok = first_ref.shape[0]
    width = sends[0].shape[1] // 2
    piece = sends[0].shape[0]
    shape = (PAIR * tok, piece * len(sends))
    both = jnp.concatenate([first_ref[...], second_ref[...]], axis=0)
    meta = both[:, 2 * width :].astype(F32)
    slot = lax.broadcasted_iota(jnp.int32, shape, 1)
    block = lax.broadcasted_iota(jnp.int32, shape, 0) // tok
    chip = slot // piece
    to_row, to_deep = here_ref[0] ^ (chip // deep), here_ref[3] ^ (chip % deep)
    device = ((to_row * PAIR + here_ref[1]) * PAIR + here_ref[2]) * deep + to_deep
    expert = (device * experts + slot // (PAIR * capacity) % experts).astype(F32)
    meant = jnp.where(slot // capacity % PAIR == block, 1.0, 0.0)
    named = jnp.zeros(shape, F32)
    weight = jnp.zeros(shape, F32)
    for k in range(top):
        hit = jnp.where(meta[:, k : k + 1] == expert, meant, 0.0)
        named = named + hit
        weight = weight + hit * meta[:, top + k : top + k + 1]
    row = lax.broadcasted_iota(jnp.int32, (PAIR * tok, PAIR * tok), 0)
    col = lax.broadcasted_iota(jnp.int32, (PAIR * tok, PAIR * tok), 1)
    earlier = dot(jnp.where(col < row, 1.0, 0.0).astype(BF16), named.astype(BF16))
    place = jnp.where(earlier == (slot % capacity).astype(F32), named, 0.0)
    place_ref[...] = place.astype(BF16)
    pick = place.T.astype(BF16)
    scale = jnp.sum((place * weight).T, axis=1, keepdims=True)
    x = dot(pick, both[:, :width]).astype(BF16)
    delta = (scale * dot(pick, both[:, width : 2 * width])).astype(BF16)
    for i, send in enumerate(sends):
        send[:, :width] = x[i * piece : (i + 1) * piece]
        send[:, width:] = delta[i * piece : (i + 1) * piece]


def load_kernel(*refs):
    count = len(refs) // 2
    sem = refs[-1]
    copies = [pltpu.make_async_copy(refs[i], refs[count + i], sem.at[i]) for i in range(count)]
    for copy in copies:
        copy.start()
    for copy in copies:
        copy.wait()


def expert_kernel(count, group, *refs):
    ins, weights, outs = refs[:count], refs[count : count + 6], refs[count + 6 : -1]
    gate, up, down, left_proj, right_proj, stored = weights
    outer_ref = refs[-1]
    experts, width, _ = gate.shape
    rank = left_proj.shape[1]
    half = count // 2
    ins = [ins[i // 2 + i % 2 * half] for i in range(count)]
    per = LANES // rank
    rows = count * group
    lane = lax.broadcasted_iota(jnp.int32, (rows, LANES), 1) // rank
    for j in range(experts):
        part = slice(j * group, (j + 1) * group)
        x = jnp.concatenate([r[part, :width] for r in ins], axis=0)
        delta = jnp.concatenate([r[part, width:] for r in ins], axis=0)
        a_gate = dot(x, gate[j])
        a_up = dot(x, up[j])
        d_hidden = dot_nt(delta, down[j])
        sig = jax.nn.sigmoid(a_gate)
        active = a_gate * sig
        hidden = (active * a_up).astype(BF16)
        grad_up = (d_hidden * active).astype(BF16)
        grad_gate = (d_hidden * a_up * sig * (1.0 + a_gate * (1.0 - sig))).astype(BF16)
        grad = (dot_nt(grad_gate, gate[j]) + dot_nt(grad_up, up[j])).astype(BF16)
        left = dot_nt(delta, left_proj[j])
        right = dot_nt(hidden, right_proj[j])
        wide = jnp.concatenate([right] * per, axis=1)
        for c in range(rank // per):
            factor = left[:, c * per : c * per + 1]
            for k in range(1, per):
                factor = jnp.where(lane == k, left[:, c * per + k : c * per + k + 1], factor)
            outer_ref[j, :, c * LANES : (c + 1) * LANES] = (factor * wide).astype(BF16)
        score = dot(outer_ref[j], stored[j]).astype(BF16)
        for i in range(count):
            here = slice(i * group, (i + 1) * group)
            to = slice((i % 2 * experts + j) * group, (i % 2 * experts + j + 1) * group)
            outs[i // 2][to, :width] = grad[here]
            outs[i // 2][to, width:] = score[here]


def part_kernel(own_ref, guest_ref, *refs):
    ins, own_keep_ref, guest_keep_ref, give_ref = refs[:-3], refs[-3], refs[-2], refs[-1]
    tok = own_keep_ref.shape[0]
    piece = ins[0].shape[0] // 2
    own = dot(own_ref[...], jnp.concatenate([r[:piece] for r in ins], axis=0))
    guest = dot(guest_ref[...], jnp.concatenate([r[piece:] for r in ins], axis=0))
    own_keep_ref[...] = own[:tok]
    guest_keep_ref[...] = guest[:tok]
    give_ref[:tok] = guest[tok:].astype(BF16)
    give_ref[tok:] = own[tok:].astype(BF16)


def join_kernel(keep_ref, more_ref, out_ref):
    out_ref[...] = (keep_ref[...] + more_ref[: keep_ref.shape[0]].astype(F32)).astype(BF16)


def final_kernel(keep_ref, more_ref, far_ref, query_ref, grad_ref, score_ref):
    width = grad_ref.shape[1]
    total = keep_ref[...] + more_ref[keep_ref.shape[0] :].astype(F32) + far_ref[...].astype(F32)
    grad_ref[...] = total[:, :width].astype(BF16)
    wanted = lax.broadcasted_iota(jnp.int32, (score_ref.shape[0], query_ref.shape[1]), 0)
    pick = jnp.where(query_ref[...] == wanted, 1.0, 0.0)
    score_ref[...] = jnp.dot(
        pick, total[:, width:], precision=lax.Precision.HIGHEST, preferred_element_type=F32
    )


VMEM = pl.BlockSpec(memory_space=pltpu.VMEM)
SMEM = pl.BlockSpec(memory_space=pltpu.SMEM)
HBM = pl.BlockSpec(memory_space=pltpu.HBM)


def in_hbm(value):
    return pltpu.with_memory_space_constraint(value, pltpu.HBM)


def call(kernel, outs, in_specs, args, scratch=(), flops=1_000_000, moved=1_000_000, limit=8 << 20):
    return pl.pallas_call(
        kernel,
        out_shape=outs,
        in_specs=in_specs,
        out_specs=jax.tree.map(lambda _: VMEM, outs),
        scratch_shapes=scratch,
        compiler_params=pltpu.CompilerParams(vmem_limit_bytes=limit),
        cost_estimate=pl.CostEstimate(flops=flops, bytes_accessed=moved, transcendentals=0),
    )(*args)


def layer(tokens, out_grad, expert_ids, gate_w, query_ids, *weights):
    weights = weights[:3] + tuple(w.transpose(0, 2, 1) for w in weights[3:5]) + weights[5:]
    weights = tuple(in_hbm(w) for w in weights)
    tok, width = tokens.shape
    top = expert_ids.shape[1]
    experts = weights[0].shape[0]
    train = weights[5].shape[2]
    row_size, deep = lax.axis_size("row"), lax.axis_size("deep")
    chips = row_size * deep
    capacity = 2 * tok // (experts * PAIR * deep)
    piece = experts * PAIR * capacity
    here = jnp.stack([lax.axis_index(a) for a in AXES]).astype(jnp.int32)
    shape = jax.ShapeDtypeStruct

    def swap(value, row=0, core=0, half=0, far=0):
        pairs = []
        for r in range(row_size):
            for c in range(PAIR):
                for h in range(PAIR):
                    for d in range(deep):
                        source = ((r * PAIR + c) * PAIR + h) * deep + d
                        target = (((r ^ row) * PAIR + (c ^ core)) * PAIR + (h ^ half)) * deep
                        pairs.append((source, target + (d ^ far)))
        return lax.ppermute(value, AXES, pairs)

    order = sorted(range(1, chips), key=lambda o: (-bin(o).count("1"), -o))

    def move(pieces, offsets):
        return {o: swap(pieces[o], row=o // deep, far=o % deep) for o in offsets}

    def exchange(pieces):
        moved = move(pieces, order)
        return [pieces[0]] + [moved[o] for o in range(1, chips)]

    def pack(first, second):
        outs = (shape((piece, 2 * width), BF16),) * chips
        outs += (shape((PAIR * tok, piece * chips), BF16),)
        kernel = functools.partial(pack_kernel, top, experts, capacity, deep)
        filled = call(kernel, outs, [SMEM, VMEM, VMEM], (here, first, second), limit=12 << 20)
        return filled[:-1], filled[-1]

    inputs = tuple(in_hbm(v) for v in (expert_ids.T, gate_w.T, tokens, out_grad))
    pay = call(
        pay_kernel,
        shape((tok, 2 * width + LANES), BF16),
        [HBM] * 4,
        inputs,
        scratch=[pltpu.VMEM(v.shape, v.dtype) for v in inputs]
        + [pltpu.SemaphoreType.DMA((len(inputs),))],
    )
    guest = swap(pay, half=1)
    other = swap(pay, core=1)
    own_send, own_place = pack(pay, other)
    own_rows = exchange(own_send)
    other = swap(guest, core=1)
    guest_send, guest_place = pack(guest, other)
    guest_rows = exchange(guest_send)
    held = pl.pallas_call(
        load_kernel,
        out_shape=tuple(pltpu.VMEM(w.shape, w.dtype) for w in weights),
        in_specs=[HBM] * len(weights),
        out_specs=(VMEM,) * len(weights),
        scratch_shapes=[pltpu.SemaphoreType.DMA((len(weights),))],
        compiler_params=pltpu.CompilerParams(vmem_limit_bytes=1 << 20),
    )(*weights)
    rows = 2 * chips * piece
    size = sum(w.size for w in weights)
    outs = call(
        functools.partial(expert_kernel, 2 * chips, PAIR * capacity),
        (shape((2 * piece, width + train), BF16),) * chips,
        [VMEM] * (2 * chips + len(weights)),
        (*own_rows, *guest_rows, *held),
        scratch=[pltpu.VMEM((experts, rows // experts, weights[5].shape[1]), BF16)],
        flops=2 * rows * size,
        moved=2 * size,
        limit=rows * (76 << 10),
    )
    keep = shape((tok, width + train), F32)
    own_keep, guest_keep, give = call(
        part_kernel,
        (keep, keep, shape((PAIR * tok, width + train), BF16)),
        [VMEM] * (2 + chips),
        (own_place, guest_place, *exchange(outs)),
    )
    more = swap(give, core=1)
    far = call(join_kernel, shape((tok, width + train), BF16), [VMEM] * 2, (guest_keep, more))
    far = swap(far, half=1)
    return call(
        final_kernel,
        (shape((tok, width), BF16), shape((QRY_DEV, train), F32)),
        [VMEM] * 4,
        (own_keep, more, far, query_ids),
    )


def solution(mesh):
    groups, line = mesh.shape["group"], mesh.shape["expert"]
    devices = mesh.devices.reshape(groups // PAIR, PAIR, PAIR, line // PAIR)
    return jax.shard_map(
        layer,
        mesh=Mesh(devices, AXES),
        in_specs=(P(AXES, None),) * 5 + (P(AXES, None, None),) * 6,
        out_specs=(P(AXES, None), P(AXES, None)),
        check_vma=False,
    )
```

```python
import functools

import jax
import jax.numpy as jnp
from jax import lax
from jax.experimental import pallas as pl
from jax.experimental.pallas import tpu as pltpu
from jax.sharding import Mesh, PartitionSpec as P


QRY_DEV = 8
PAIR = 2
LANES = 128
F32 = jnp.float32
BF16 = jnp.bfloat16
NT = (((1,), (1,)), ((), ()))
AXES = ("row", "core", "half", "deep")


def dot(a, b):
    return jnp.dot(a, b, preferred_element_type=F32)


def dot_nt(a, b):
    return lax.dot_general(a, b, NT, preferred_element_type=F32)


def pay_kernel(
    ids_hbm, w_hbm, query_hbm, x_hbm, g_hbm, pay_ref, ids_ref, w_ref, query_ref, x_ref, g_ref, sem
):
    top, tok = ids_ref.shape
    width = x_ref.shape[1]
    pairs = (
        (ids_hbm, ids_ref),
        (w_hbm, w_ref),
        (query_hbm, query_ref),
        (x_hbm, x_ref),
        (g_hbm, g_ref),
    )
    copies = [pltpu.make_async_copy(a, b, sem.at[i]) for i, (a, b) in enumerate(pairs)]
    for copy in copies:
        copy.start()
    for copy in copies[:3]:
        copy.wait()
    parts = [ids_ref[...].astype(F32), w_ref[...].astype(F32), query_ref[...].astype(F32)]
    flat = jnp.concatenate(parts + [jnp.zeros((LANES - 2 * top - 1, tok), F32)], axis=0)
    flat = jnp.concatenate([flat, jnp.zeros((LANES, LANES - tok), F32)], axis=1)
    pay_ref[:, 2 * width :] = flat.T[:tok, :].astype(BF16)
    copies[3].wait()
    pay_ref[:, :width] = x_ref[...]
    copies[4].wait()
    pay_ref[:, width : 2 * width] = g_ref[...]


def pack_kernel(top, experts, capacity, deep, here_ref, first_ref, second_ref, *outs):
    place_ref, tally_ref, sends = outs[-2], outs[-1], outs[:-2]
    tok = first_ref.shape[0]
    width = sends[0].shape[1] // 2
    piece = sends[0].shape[0]
    shape = (PAIR * tok, piece * len(sends))
    both = jnp.concatenate([first_ref[...], second_ref[...]], axis=0)
    meta = both[:, 2 * width :].astype(F32)
    slot = lax.broadcasted_iota(jnp.int32, shape, 1)
    block = lax.broadcasted_iota(jnp.int32, shape, 0) // tok
    chip = slot // piece
    to_row, to_deep = here_ref[0] ^ (chip // deep), here_ref[3] ^ (chip % deep)
    device = ((to_row * PAIR + here_ref[1]) * PAIR + here_ref[2]) * deep + to_deep
    expert = (device * experts + slot // (PAIR * capacity) % experts).astype(F32)
    meant = jnp.where(slot // capacity % PAIR == block, 1.0, 0.0)
    named = jnp.zeros(shape, F32)
    weight = jnp.zeros(shape, F32)
    for k in range(top):
        hit = jnp.where(meta[:, k : k + 1] == expert, meant, 0.0)
        named = named + hit
        weight = weight + hit * meta[:, top + k : top + k + 1]
    row = lax.broadcasted_iota(jnp.int32, (PAIR * tok, PAIR * tok), 0)
    col = lax.broadcasted_iota(jnp.int32, (PAIR * tok, PAIR * tok), 1)
    earlier = dot(jnp.where(col < row, 1.0, 0.0).astype(BF16), named.astype(BF16))
    place = jnp.where(earlier == (slot % capacity).astype(F32), named, 0.0)
    place_ref[...] = place.astype(BF16)
    asked = lax.broadcasted_iota(jnp.int32, (PAIR * tok, LANES), 1)
    whose = lax.broadcasted_iota(jnp.int32, (PAIR * tok, LANES), 0) // tok
    query = meta[:, 2 * top : 2 * top + 1] + (whose * QRY_DEV).astype(F32)
    asked = jnp.where(query == asked.astype(F32), 1.0, 0.0)
    tally = dot(asked.T[: PAIR * QRY_DEV].astype(BF16), place.astype(BF16))
    tally_ref[...] = tally.astype(BF16)
    pick = place.T.astype(BF16)
    scale = jnp.sum((place * weight).T, axis=1, keepdims=True)
    x = dot(pick, both[:, :width]).astype(BF16)
    delta = (scale * dot(pick, both[:, width : 2 * width])).astype(BF16)
    for i, send in enumerate(sends):
        send[:, :width] = x[i * piece : (i + 1) * piece]
        send[:, width:] = delta[i * piece : (i + 1) * piece]


def load_kernel(*refs):
    count = len(refs) // 2
    sem = refs[-1]
    copies = [pltpu.make_async_copy(refs[i], refs[count + i], sem.at[i]) for i in range(count)]
    for copy in copies:
        copy.start()
    for copy in copies:
        copy.wait()


def expert_kernel(count, group, *refs):
    ins, weights, outs = refs[:count], refs[count : count + 6], refs[count + 6 : -1]
    gate, up, down, left_proj, right_proj, stored = weights
    outer_ref = refs[-1]
    experts, width, _ = gate.shape
    rank = left_proj.shape[1]
    half = count // 2
    ins = [ins[i // 2 + i % 2 * half] for i in range(count)]
    per = LANES // rank
    rows = count * group
    lane = lax.broadcasted_iota(jnp.int32, (rows, LANES), 1) // rank

    def front(j):
        part = slice(j * group, (j + 1) * group)
        x = jnp.concatenate([r[part, :width] for r in ins], axis=0)
        delta = jnp.concatenate([r[part, width:] for r in ins], axis=0)
        left = dot_nt(delta, left_proj[j])
        return dot(x, gate[j]), dot(x, up[j]), dot_nt(delta, down[j]), left

    def middle(j, a_gate, a_up, d_hidden, left):
        sig = jax.nn.sigmoid(a_gate)
        active = a_gate * sig
        hidden = (active * a_up).astype(BF16)
        right = dot_nt(hidden, right_proj[j])
        grad_up = (d_hidden * active).astype(BF16)
        grad_gate = (d_hidden * a_up * sig * (1.0 + a_gate * (1.0 - sig))).astype(BF16)
        return grad_gate, grad_up, left, right

    def outers(j, left, right):
        wide = jnp.concatenate([right] * per, axis=1)
        for c in range(rank // per):
            factor = left[:, c * per : c * per + 1]
            for k in range(1, per):
                factor = jnp.where(lane == k, left[:, c * per + k : c * per + k + 1], factor)
            outer_ref[j, :, c * LANES : (c + 1) * LANES] = (factor * wide).astype(BF16)

    def put(j, value, columns):
        value = value.astype(BF16)
        for i in range(count):
            to = slice((i % 2 * experts + j) * group, (i % 2 * experts + j + 1) * group)
            outs[i // 2][to, columns] = value[i * group : (i + 1) * group]

    def grads(j, grad_gate, grad_up):
        put(j, dot_nt(grad_gate, gate[j]) + dot_nt(grad_up, up[j]), slice(0, width))

    def scores(j):
        put(j, dot(outer_ref[j], stored[j]), slice(width, width + stored.shape[2]))

    every = range(experts)
    second = []
    for j in every:
        second.append(middle(j, *front(j)))
    for j in every:
        outers(j, *second[j][2:])
        grads(j, *second[j][:2])
        scores(j)


def part_kernel(own_ref, own_tally_ref, guest_ref, guest_tally_ref, *refs):
    ins, own_keep_ref, guest_keep_ref, give_ref = refs[:-3], refs[-3], refs[-2], refs[-1]
    tok, span = own_keep_ref.shape
    width = span - LANES
    piece = ins[0].shape[0] // 2

    def token_sums(place_ref, tally_ref, part):
        grads = jnp.concatenate([r[part, :width] for r in ins], axis=0)
        scores = jnp.concatenate([r[part, width:] for r in ins], axis=0)
        total, tally = dot(place_ref[...], grads), dot(tally_ref[...], scores)

        def fold(block):
            rows = tally[block * QRY_DEV : (block + 1) * QRY_DEV]
            return jnp.concatenate(
                [rows[:, i : i + LANES] for i in range(0, rows.shape[1], LANES)], axis=0
            )

        return total, fold

    own, own_fold = token_sums(own_ref, own_tally_ref, slice(0, piece))
    guest, guest_fold = token_sums(guest_ref, guest_tally_ref, slice(piece, 2 * piece))
    own_keep_ref[:, :width] = own[:tok]
    own_keep_ref[:, width:] = own_fold(0)
    guest_keep_ref[:, :width] = guest[:tok]
    guest_keep_ref[:, width:] = guest_fold(0)
    give_ref[:tok, :width] = guest[tok:].astype(BF16)
    give_ref[:tok, width:] = guest_fold(1).astype(BF16)
    give_ref[tok:, :width] = own[tok:].astype(BF16)
    give_ref[tok:, width:] = own_fold(1).astype(BF16)


def join_kernel(keep_ref, more_ref, out_ref):
    out_ref[...] = (keep_ref[...] + more_ref[: keep_ref.shape[0]].astype(F32)).astype(BF16)


def final_kernel(keep_ref, more_ref, far_ref, grad_ref, score_ref):
    tok, width = grad_ref.shape
    total = keep_ref[...] + more_ref[tok:].astype(F32) + far_ref[...].astype(F32)
    grad_ref[...] = total[:, :width].astype(BF16)
    for i in range(tok // QRY_DEV):
        part = total[i * QRY_DEV : (i + 1) * QRY_DEV, width:]
        score_ref[:, i * LANES : (i + 1) * LANES] = part


VMEM = pl.BlockSpec(memory_space=pltpu.VMEM)
SMEM = pl.BlockSpec(memory_space=pltpu.SMEM)
HBM = pl.BlockSpec(memory_space=pltpu.HBM)


def in_hbm(value):
    return pltpu.with_memory_space_constraint(value, pltpu.HBM)


def call(kernel, outs, in_specs, args, scratch=(), flops=1_000_000, moved=1_000_000, limit=8 << 20):
    return pl.pallas_call(
        kernel,
        out_shape=outs,
        in_specs=in_specs,
        out_specs=jax.tree.map(lambda _: VMEM, outs),
        scratch_shapes=scratch,
        compiler_params=pltpu.CompilerParams(vmem_limit_bytes=limit),
        cost_estimate=pl.CostEstimate(flops=flops, bytes_accessed=moved, transcendentals=0),
    )(*args)


def layer(tokens, out_grad, expert_ids, gate_w, query_ids, *weights):
    weights = weights[:3] + tuple(w.transpose(0, 2, 1) for w in weights[3:5]) + weights[5:]
    weights = tuple(in_hbm(w) for w in weights)
    tok, width = tokens.shape
    top = expert_ids.shape[1]
    experts = weights[0].shape[0]
    train = weights[5].shape[2]
    row_size, deep = lax.axis_size("row"), lax.axis_size("deep")
    chips = row_size * deep
    capacity = 2 * tok // (experts * PAIR * deep)
    piece = experts * PAIR * capacity
    here = jnp.stack([lax.axis_index(a) for a in AXES]).astype(jnp.int32)
    shape = jax.ShapeDtypeStruct

    def swap(value, row=0, core=0, half=0, far=0):
        pairs = []
        for r in range(row_size):
            for c in range(PAIR):
                for h in range(PAIR):
                    for d in range(deep):
                        source = ((r * PAIR + c) * PAIR + h) * deep + d
                        target = (((r ^ row) * PAIR + (c ^ core)) * PAIR + (h ^ half)) * deep
                        pairs.append((source, target + (d ^ far)))
        return lax.ppermute(value, AXES, pairs)

    order = sorted(range(1, chips), key=lambda o: (-bin(o).count("1"), -o))

    def move(pieces, offsets):
        return {o: swap(pieces[o], row=o // deep, far=o % deep) for o in offsets}

    def exchange(pieces):
        moved = move(pieces, order)
        return [pieces[0]] + [moved[o] for o in range(1, chips)]

    def pack(first, second):
        outs = (shape((piece, 2 * width), BF16),) * chips
        outs += (shape((PAIR * tok, piece * chips), BF16),)
        outs += (shape((PAIR * QRY_DEV, piece * chips), BF16),)
        kernel = functools.partial(pack_kernel, top, experts, capacity, deep)
        filled = call(kernel, outs, [SMEM, VMEM, VMEM], (here, first, second), limit=12 << 20)
        return filled[:-2], filled[-2:]

    inputs = tuple(in_hbm(v) for v in (expert_ids.T, gate_w.T, query_ids, tokens, out_grad))
    pay = call(
        pay_kernel,
        shape((tok, 2 * width + LANES), BF16),
        [HBM] * len(inputs),
        inputs,
        scratch=[pltpu.VMEM(v.shape, v.dtype) for v in inputs]
        + [pltpu.SemaphoreType.DMA((len(inputs),))],
    )
    guest = swap(pay, half=1)
    other = swap(pay, core=1)
    own_send, own_place = pack(pay, other)
    own_rows = exchange(own_send)
    other = swap(guest, core=1)
    guest_send, guest_place = pack(guest, other)
    guest_rows = exchange(guest_send)
    held = pl.pallas_call(
        load_kernel,
        out_shape=tuple(pltpu.VMEM(w.shape, w.dtype) for w in weights),
        in_specs=[HBM] * len(weights),
        out_specs=(VMEM,) * len(weights),
        scratch_shapes=[pltpu.SemaphoreType.DMA((len(weights),))],
        compiler_params=pltpu.CompilerParams(vmem_limit_bytes=1 << 20),
    )(*weights)
    rows = 2 * chips * piece
    size = sum(w.size for w in weights)
    outs = call(
        functools.partial(expert_kernel, 2 * chips, PAIR * capacity),
        (shape((2 * piece, width + train), BF16),) * chips,
        [VMEM] * (2 * chips + len(weights)),
        (*own_rows, *guest_rows, *held),
        scratch=[pltpu.VMEM((experts, rows // experts, weights[5].shape[1]), BF16)],
        flops=2 * rows * size,
        moved=2 * size,
        limit=rows * (76 << 10),
    )
    assert QRY_DEV * train == tok * LANES
    keep = shape((tok, width + LANES), F32)
    own_keep, guest_keep, give = call(
        part_kernel,
        (keep, keep, shape((PAIR * tok, width + LANES), BF16)),
        [VMEM] * (4 + chips),
        (*own_place, *guest_place, *exchange(outs)),
    )
    more = swap(give, core=1)
    far = call(join_kernel, shape((tok, width + LANES), BF16), [VMEM] * 2, (guest_keep, more))
    far = swap(far, half=1)
    return call(
        final_kernel,
        (shape((tok, width), BF16), shape((QRY_DEV, train), F32)),
        [VMEM] * 3,
        (own_keep, more, far),
    )


def solution(mesh):
    groups, line = mesh.shape["group"], mesh.shape["expert"]
    devices = mesh.devices.reshape(groups // PAIR, PAIR, PAIR, line // PAIR)
    return jax.shard_map(
        layer,
        mesh=Mesh(devices, AXES),
        in_specs=(P(AXES, None),) * 5 + (P(AXES, None, None),) * 6,
        out_specs=(P(AXES, None), P(AXES, None)),
        check_vma=False,
    )
```

```python
import functools

import jax
import jax.numpy as jnp
from jax import lax
from jax.experimental import pallas as pl
from jax.experimental.pallas import tpu as pltpu
from jax.sharding import Mesh, PartitionSpec as P


QRY_DEV = 8
PAIR = 2
LANES = 128
F32 = jnp.float32
BF16 = jnp.bfloat16
NT = (((1,), (1,)), ((), ()))
AXES = ("row", "core", "half", "deep")


def dot(a, b):
    return jnp.dot(a, b, preferred_element_type=F32)


def dot_nt(a, b):
    return lax.dot_general(a, b, NT, preferred_element_type=F32)


def pay_kernel(
    ids_hbm, w_hbm, query_hbm, x_hbm, g_hbm, pay_ref, ids_ref, w_ref, query_ref, x_ref, g_ref, sem
):
    top, tok = ids_ref.shape
    width = x_ref.shape[1]
    pairs = (
        (ids_hbm, ids_ref),
        (w_hbm, w_ref),
        (query_hbm, query_ref),
        (x_hbm, x_ref),
        (g_hbm, g_ref),
    )
    copies = [pltpu.make_async_copy(a, b, sem.at[i]) for i, (a, b) in enumerate(pairs)]
    for copy in copies:
        copy.start()
    for copy in copies[:3]:
        copy.wait()
    parts = [ids_ref[...].astype(F32), w_ref[...].astype(F32), query_ref[...].astype(F32)]
    flat = jnp.concatenate(parts + [jnp.zeros((LANES - 2 * top - 1, tok), F32)], axis=0)
    flat = jnp.concatenate([flat, jnp.zeros((LANES, LANES - tok), F32)], axis=1)
    pay_ref[:, 2 * width :] = flat.T[:tok, :].astype(BF16)
    copies[3].wait()
    pay_ref[:, :width] = x_ref[...]
    copies[4].wait()
    pay_ref[:, width : 2 * width] = g_ref[...]


def pack_kernel(top, experts, capacity, deep, first_ref, second_ref, *outs):
    place_ref, tally_ref, sends = outs[-2], outs[-1], outs[:-2]
    tok = first_ref.shape[0]
    width = sends[0].shape[1] // 2
    piece = sends[0].shape[0]
    shape = (PAIR * tok, piece * len(sends))
    both = jnp.concatenate([first_ref[...], second_ref[...]], axis=0)
    meta = both[:, 2 * width :].astype(F32)
    slot = lax.broadcasted_iota(jnp.int32, shape, 1)
    block = lax.broadcasted_iota(jnp.int32, shape, 0) // tok
    chip = slot // piece
    here = [lax.axis_index(a) for a in AXES]
    to_row, to_deep = here[0] ^ (chip // deep), here[3] ^ (chip % deep)
    device = ((to_row * PAIR + here[1]) * PAIR + here[2]) * deep + to_deep
    expert = (device * experts + slot // (PAIR * capacity) % experts).astype(F32)
    meant = jnp.where(slot // capacity % PAIR == block, 1.0, 0.0)
    named = jnp.zeros(shape, F32)
    weight = jnp.zeros(shape, F32)
    for k in range(top):
        hit = jnp.where(meta[:, k : k + 1] == expert, meant, 0.0)
        named = named + hit
        weight = weight + hit * meta[:, top + k : top + k + 1]
    row = lax.broadcasted_iota(jnp.int32, (PAIR * tok, PAIR * tok), 0)
    col = lax.broadcasted_iota(jnp.int32, (PAIR * tok, PAIR * tok), 1)
    earlier = dot(jnp.where(col < row, 1.0, 0.0).astype(BF16), named.astype(BF16))
    place = jnp.where(earlier == (slot % capacity).astype(F32), named, 0.0)
    place_ref[...] = place.astype(BF16)
    asked = lax.broadcasted_iota(jnp.int32, (PAIR * tok, LANES), 1)
    whose = lax.broadcasted_iota(jnp.int32, (PAIR * tok, LANES), 0) // tok
    query = meta[:, 2 * top : 2 * top + 1] + (whose * QRY_DEV).astype(F32)
    asked = jnp.where(query == asked.astype(F32), 1.0, 0.0)
    tally = dot(asked.T[: PAIR * QRY_DEV].astype(BF16), place.astype(BF16))
    tally_ref[...] = tally.astype(BF16)
    pick = place.T.astype(BF16)
    scale = jnp.sum((place * weight).T, axis=1, keepdims=True)
    x = dot(pick, both[:, :width]).astype(BF16)
    delta = (scale * dot(pick, both[:, width : 2 * width])).astype(BF16)
    for i, send in enumerate(sends):
        send[:, :width] = x[i * piece : (i + 1) * piece]
        send[:, width:] = delta[i * piece : (i + 1) * piece]


def load_kernel(*refs):
    count = len(refs) // 2
    sem = refs[-1]
    copies = [pltpu.make_async_copy(refs[i], refs[count + i], sem.at[i]) for i in range(count)]
    for copy in copies:
        copy.start()
    for copy in copies:
        copy.wait()


def expert_kernel(count, group, deep, *refs):
    ins, weights = refs[:count], refs[count : count + 6]
    own_ref, outs, stage_ref = refs[count + 6], refs[count + 7 : -2], refs[-2]
    me = lax.axis_index("row") * deep + lax.axis_index("deep")
    gate, up, down, left_proj, right_proj, stored = weights
    outer_ref = refs[-1]
    experts, width, _ = gate.shape
    rank = left_proj.shape[1]
    half = count // 2
    per = LANES // rank
    rows = count * group
    lane = lax.broadcasted_iota(jnp.int32, (rows, LANES), 1) // rank

    def front(j):
        part = slice(j * group, (j + 1) * group)
        x = jnp.concatenate([r[part, :width] for r in ins], axis=0)
        delta = jnp.concatenate([r[part, width:] for r in ins], axis=0)
        left = dot_nt(delta, left_proj[j])
        return dot(x, gate[j]), dot(x, up[j]), dot_nt(delta, down[j]), left

    def middle(j, a_gate, a_up, d_hidden, left):
        sig = jax.nn.sigmoid(a_gate)
        active = a_gate * sig
        hidden = (active * a_up).astype(BF16)
        right = dot_nt(hidden, right_proj[j])
        grad_up = (d_hidden * active).astype(BF16)
        grad_gate = (d_hidden * a_up * sig * (1.0 + a_gate * (1.0 - sig))).astype(BF16)
        return grad_gate, grad_up, left, right

    def outers(j, left, right):
        wide = jnp.concatenate([right] * per, axis=1)
        for c in range(rank // per):
            factor = left[:, c * per : c * per + 1]
            for k in range(1, per):
                factor = jnp.where(lane == k, left[:, c * per + k : c * per + k + 1], factor)
            outer_ref[j, :, c * LANES : (c + 1) * LANES] = (factor * wide).astype(BF16)

    def put(j, value, columns):
        value = value.astype(BF16)
        part = slice(j * group, (j + 1) * group)
        for i in range(half):
            stage_ref[i, part, columns] = value[i * group : (i + 1) * group]
        for i in range(half):
            outs[i][part, columns] = value[(half + i) * group : (half + i + 1) * group]

    def grads(j, grad_gate, grad_up):
        put(j, dot_nt(grad_gate, gate[j]) + dot_nt(grad_up, up[j]), slice(0, width))

    def scores(j):
        put(j, dot(outer_ref[j], stored[j]), slice(width, width + stored.shape[2]))

    every = range(experts)
    second = []
    for j in every:
        second.append(middle(j, *front(j)))
    for j in every:
        outers(j, *second[j][2:])
        grads(j, *second[j][:2])
        scores(j)
    for i in range(half):
        own_ref[i ^ me] = stage_ref[i]


def token_sums(place_ref, tally_ref, ins, keep_ref, give_ref):
    tok, span = keep_ref.shape
    width = span - LANES
    rows = jnp.concatenate(ins, axis=0)
    total, tally = dot(place_ref[...], rows[:, :width]), dot(tally_ref[...], rows[:, width:])

    def fold(block):
        part = tally[block * QRY_DEV : (block + 1) * QRY_DEV]
        pieces = [part[:, i : i + LANES] for i in range(0, part.shape[1], LANES)]
        return jnp.concatenate(pieces, axis=0)

    keep_ref[:, :width] = total[:tok]
    keep_ref[:, width:] = fold(0)
    give_ref[:, :width] = total[tok:].astype(BF16)
    give_ref[:, width:] = fold(1).astype(BF16)


def guest_part_kernel(place_ref, tally_ref, *refs):
    token_sums(place_ref, tally_ref, [r[...] for r in refs[:-2]], *refs[-2:])


def own_part_kernel(deep, place_ref, tally_ref, rows_ref, keep_ref, give_ref):
    me = lax.axis_index("row") * deep + lax.axis_index("deep")
    ins = [rows_ref[i ^ me] for i in range(rows_ref.shape[0])]
    token_sums(place_ref, tally_ref, ins, keep_ref, give_ref)


def join_kernel(keep_ref, more_ref, out_ref):
    out_ref[...] = (keep_ref[...] + more_ref[...].astype(F32)).astype(BF16)


def final_kernel(keep_ref, more_ref, far_ref, grad_ref, score_ref):
    tok, width = grad_ref.shape
    total = keep_ref[...] + more_ref[...].astype(F32) + far_ref[...].astype(F32)
    grad_ref[...] = total[:, :width].astype(BF16)
    for i in range(tok // QRY_DEV):
        part = total[i * QRY_DEV : (i + 1) * QRY_DEV, width:]
        score_ref[:, i * LANES : (i + 1) * LANES] = part


VMEM = pl.BlockSpec(memory_space=pltpu.VMEM)
HBM = pl.BlockSpec(memory_space=pltpu.HBM)


def in_hbm(value):
    return pltpu.with_memory_space_constraint(value, pltpu.HBM)


def call(kernel, outs, in_specs, args, scratch=(), flops=1_000_000, moved=1_000_000, limit=8 << 20):
    return pl.pallas_call(
        kernel,
        out_shape=outs,
        in_specs=in_specs,
        out_specs=jax.tree.map(lambda _: VMEM, outs),
        scratch_shapes=scratch,
        compiler_params=pltpu.CompilerParams(vmem_limit_bytes=limit),
        cost_estimate=pl.CostEstimate(flops=flops, bytes_accessed=moved, transcendentals=0),
    )(*args)


def layer(tokens, out_grad, expert_ids, gate_w, query_ids, *weights):
    weights = weights[:3] + tuple(w.transpose(0, 2, 1) for w in weights[3:5]) + weights[5:]
    weights = tuple(in_hbm(w) for w in weights)
    tok, width = tokens.shape
    top = expert_ids.shape[1]
    experts = weights[0].shape[0]
    train = weights[5].shape[2]
    row_size, deep = lax.axis_size("row"), lax.axis_size("deep")
    chips = row_size * deep
    capacity = 2 * tok // (experts * PAIR * deep)
    piece = experts * PAIR * capacity
    shape = jax.ShapeDtypeStruct

    def swap(value, row=0, core=0, half=0, far=0):
        pairs = []
        for r in range(row_size):
            for c in range(PAIR):
                for h in range(PAIR):
                    for d in range(deep):
                        source = ((r * PAIR + c) * PAIR + h) * deep + d
                        target = (((r ^ row) * PAIR + (c ^ core)) * PAIR + (h ^ half)) * deep
                        pairs.append((source, target + (d ^ far)))
        return lax.ppermute(value, AXES, pairs)

    order = sorted(range(1, chips), key=lambda o: (-bin(o).count("1"), -o))

    def move(pieces, offsets):
        return {o: swap(pieces[o], row=o // deep, far=o % deep) for o in offsets}

    def exchange(pieces):
        moved = move(pieces, order)
        return [pieces[0]] + [moved[o] for o in range(1, chips)]

    def pack(first, second):
        outs = (shape((piece, 2 * width), BF16),) * chips
        outs += (shape((PAIR * tok, piece * chips), BF16),)
        outs += (shape((PAIR * QRY_DEV, piece * chips), BF16),)
        kernel = functools.partial(pack_kernel, top, experts, capacity, deep)
        filled = call(kernel, outs, [VMEM, VMEM], (first, second), limit=12 << 20)
        return filled[:-2], filled[-2:]

    inputs = tuple(in_hbm(v) for v in (expert_ids.T, gate_w.T, query_ids, tokens, out_grad))
    pay = call(
        pay_kernel,
        shape((tok, 2 * width + LANES), BF16),
        [HBM] * len(inputs),
        inputs,
        scratch=[pltpu.VMEM(v.shape, v.dtype) for v in inputs]
        + [pltpu.SemaphoreType.DMA((len(inputs),))],
    )
    guest = swap(pay, half=1)
    other = swap(pay, core=1)
    own_send, own_place = pack(pay, other)
    own_rows = exchange(own_send)
    other = swap(guest, core=1)
    guest_send, guest_place = pack(guest, other)
    guest_rows = exchange(guest_send)
    held = pl.pallas_call(
        load_kernel,
        out_shape=tuple(pltpu.VMEM(w.shape, w.dtype) for w in weights),
        in_specs=[HBM] * len(weights),
        out_specs=(VMEM,) * len(weights),
        scratch_shapes=[pltpu.SemaphoreType.DMA((len(weights),))],
        compiler_params=pltpu.CompilerParams(vmem_limit_bytes=1 << 20),
    )(*weights)
    rows = 2 * chips * piece
    size = sum(w.size for w in weights)
    outs = call(
        functools.partial(expert_kernel, 2 * chips, PAIR * capacity, deep),
        (shape((chips, piece, width + train), BF16),)
        + (shape((piece, width + train), BF16),) * chips,
        [VMEM] * (2 * chips + len(weights)),
        (*own_rows, *guest_rows, *held),
        scratch=[
            pltpu.VMEM((chips, piece, width + train), BF16),
            pltpu.VMEM((experts, rows // experts, weights[5].shape[1]), BF16),
        ],
        flops=2 * rows * size,
        moved=2 * size,
        limit=rows * (76 << 10),
    )
    assert QRY_DEV * train == tok * LANES
    guest_back = exchange(outs[1:])
    own_back = lax.all_to_all(outs[0], ("row", "deep"), 0, 0, tiled=True)
    sums = (shape((tok, width + LANES), F32), shape((tok, width + LANES), BF16))
    guest_keep, guest_give = call(
        guest_part_kernel, sums, [VMEM] * (2 + chips), (*guest_place, *guest_back)
    )
    more = swap(guest_give, core=1)
    far = call(join_kernel, sums[1], [VMEM] * 2, (guest_keep, more))
    far = swap(far, half=1)
    own_keep, own_give = call(
        functools.partial(own_part_kernel, deep),
        sums,
        [VMEM] * 3,
        (*own_place, own_back),
    )
    more = swap(own_give, core=1)
    return call(
        final_kernel,
        (shape((tok, width), BF16), shape((QRY_DEV, train), F32)),
        [VMEM] * 3,
        (own_keep, more, far),
    )


def solution(mesh):
    groups, line = mesh.shape["group"], mesh.shape["expert"]
    devices = mesh.devices.reshape(groups // PAIR, PAIR, PAIR, line // PAIR)
    return jax.shard_map(
        layer,
        mesh=Mesh(devices, AXES),
        in_specs=(P(AXES, None),) * 5 + (P(AXES, None, None),) * 6,
        out_specs=(P(AXES, None), P(AXES, None)),
        check_vma=False,
    )
```

```python
import functools

import jax
import jax.numpy as jnp
from jax import lax
from jax.experimental import pallas as pl
from jax.experimental.pallas import tpu as pltpu
from jax.sharding import Mesh, PartitionSpec as P


QRY_DEV = 8
PAIR = 2
LANES = 128
F32 = jnp.float32
BF16 = jnp.bfloat16
NT = (((1,), (1,)), ((), ()))
AXES = ("row", "core", "half", "deep")


def dot(a, b):
    return jnp.dot(a, b, preferred_element_type=F32)


def dot_nt(a, b):
    return lax.dot_general(a, b, NT, preferred_element_type=F32)


def pay_kernel(
    ids_hbm, w_hbm, query_hbm, x_hbm, g_hbm, pay_ref, ids_ref, w_ref, query_ref, sem
):
    top, tok = ids_ref.shape
    width = x_hbm.shape[1]
    pairs = (
        (ids_hbm, ids_ref),
        (w_hbm, w_ref),
        (query_hbm, query_ref),
        (x_hbm, pay_ref.at[:, :width]),
        (g_hbm, pay_ref.at[:, width : 2 * width]),
    )
    copies = [pltpu.make_async_copy(a, b, sem.at[i]) for i, (a, b) in enumerate(pairs)]
    for copy in copies:
        copy.start()
    for copy in copies[:3]:
        copy.wait()
    parts = [ids_ref[...].astype(F32), w_ref[...].astype(F32), query_ref[...].astype(F32)]
    flat = jnp.concatenate(parts + [jnp.zeros((LANES - 2 * top - 1, tok), F32)], axis=0)
    flat = jnp.concatenate([flat, jnp.zeros((LANES, LANES - tok), F32)], axis=1)
    pay_ref[:, 2 * width :] = flat.T[:tok, :].astype(BF16)
    for copy in copies[3:]:
        copy.wait()


def pack_kernel(top, experts, capacity, deep, first_ref, second_ref, *outs):
    place_ref, tally_ref, sends = outs[-2], outs[-1], outs[:-2]
    tok = first_ref.shape[0]
    width = sends[0].shape[1] // 2
    piece = sends[0].shape[0]
    shape = (PAIR * tok, piece * len(sends))
    both = jnp.concatenate([first_ref[...], second_ref[...]], axis=0)
    meta = both[:, 2 * width :].astype(F32)
    slot = lax.broadcasted_iota(jnp.int32, shape, 1)
    block = lax.broadcasted_iota(jnp.int32, shape, 0) // tok
    chip = slot // piece
    here = [lax.axis_index(a) for a in AXES]
    to_row, to_deep = here[0] ^ (chip // deep), here[3] ^ (chip % deep)
    device = ((to_row * PAIR + here[1]) * PAIR + here[2]) * deep + to_deep
    expert = (device * experts + slot // (PAIR * capacity) % experts).astype(F32)
    meant = jnp.where(slot // capacity % PAIR == block, 1.0, 0.0)
    named = jnp.zeros(shape, F32)
    weight = jnp.zeros(shape, F32)
    for k in range(top):
        hit = jnp.where(meta[:, k : k + 1] == expert, meant, 0.0)
        named = named + hit
        weight = weight + hit * meta[:, top + k : top + k + 1]
    row = lax.broadcasted_iota(jnp.int32, (PAIR * tok, PAIR * tok), 0)
    col = lax.broadcasted_iota(jnp.int32, (PAIR * tok, PAIR * tok), 1)
    earlier = dot(jnp.where(col < row, 1.0, 0.0).astype(BF16), named.astype(BF16))
    place = jnp.where(earlier == (slot % capacity).astype(F32), named, 0.0)
    place_ref[...] = place.astype(BF16)
    asked = lax.broadcasted_iota(jnp.int32, (PAIR * tok, LANES), 1)
    whose = lax.broadcasted_iota(jnp.int32, (PAIR * tok, LANES), 0) // tok
    query = meta[:, 2 * top : 2 * top + 1] + (whose * QRY_DEV).astype(F32)
    asked = jnp.where(query == asked.astype(F32), 1.0, 0.0)
    tally = dot(asked.T[: PAIR * QRY_DEV].astype(BF16), place.astype(BF16))
    tally_ref[...] = tally.astype(BF16)
    pick = place.T.astype(BF16)
    scale = jnp.sum((place * weight).T, axis=1, keepdims=True)
    x = dot(pick, both[:, :width]).astype(BF16)
    delta = (scale * dot(pick, both[:, width : 2 * width])).astype(BF16)
    for i, send in enumerate(sends):
        send[:, :width] = x[i * piece : (i + 1) * piece]
        send[:, width:] = delta[i * piece : (i + 1) * piece]


def load_kernel(*refs):
    count = len(refs) // 2
    sem = refs[-1]
    copies = [pltpu.make_async_copy(refs[i], refs[count + i], sem.at[i]) for i in range(count)]
    for copy in copies:
        copy.start()
    for copy in copies:
        copy.wait()


def expert_kernel(count, group, deep, *refs):
    ins, weights = refs[:count], refs[count : count + 6]
    own_ref, outs, stage_ref = refs[count + 6], refs[count + 7 : -3], refs[-3]
    sem = refs[-1]
    me = lax.axis_index("row") * deep + lax.axis_index("deep")
    gate, up, down, left_proj, right_proj, stored = weights
    outer_ref = refs[-2]
    experts, width, _ = gate.shape
    rank = left_proj.shape[1]
    half = count // 2
    per = LANES // rank
    rows = count * group
    lane = lax.broadcasted_iota(jnp.int32, (rows, LANES), 1) // rank

    def front(j):
        part = slice(j * group, (j + 1) * group)
        x = jnp.concatenate([r[part, :width] for r in ins], axis=0)
        delta = jnp.concatenate([r[part, width:] for r in ins], axis=0)
        left = dot_nt(delta, left_proj[j])
        return dot(x, gate[j]), dot(x, up[j]), dot_nt(delta, down[j]), left

    def middle(j, a_gate, a_up, d_hidden, left):
        sig = jax.nn.sigmoid(a_gate)
        active = a_gate * sig
        hidden = (active * a_up).astype(BF16)
        right = dot_nt(hidden, right_proj[j])
        grad_up = (d_hidden * active).astype(BF16)
        grad_gate = (d_hidden * a_up * sig * (1.0 + a_gate * (1.0 - sig))).astype(BF16)
        return grad_gate, grad_up, left, right

    def outers(j, left, right):
        wide = jnp.concatenate([right] * per, axis=1)
        for c in range(rank // per):
            factor = left[:, c * per : c * per + 1]
            for k in range(1, per):
                factor = jnp.where(lane == k, left[:, c * per + k : c * per + k + 1], factor)
            outer_ref[j, :, c * LANES : (c + 1) * LANES] = (factor * wide).astype(BF16)

    def put(j, value, columns):
        value = value.astype(BF16)
        part = slice(j * group, (j + 1) * group)
        for i in range(half):
            stage_ref[i, part, columns] = value[i * group : (i + 1) * group]
        for i in range(half):
            outs[i][part, columns] = value[(half + i) * group : (half + i + 1) * group]

    def grads(j, grad_gate, grad_up):
        put(j, dot_nt(grad_gate, gate[j]) + dot_nt(grad_up, up[j]), slice(0, width))

    def scores(j):
        put(j, dot(outer_ref[j], stored[j]), slice(width, width + stored.shape[2]))

    def send(step, columns):
        copies = []
        for i in range(half):
            source, target = stage_ref.at[i, :, columns], own_ref.at[i ^ me, :, columns]
            copies.append(pltpu.make_async_copy(source, target, sem.at[step, i]))
            copies[-1].start()
        return copies

    every = range(experts)
    second = []
    for j in every:
        second.append(middle(j, *front(j)))
    for j in every:
        outers(j, *second[j][2:])
        grads(j, *second[j][:2])
        if j == experts - 1:
            copies = send(0, slice(0, width))
        scores(j)
    copies += send(1, slice(width, width + stored.shape[2]))
    for copy in copies:
        copy.wait()


def token_sums(place_ref, tally_ref, ins, keep_ref, give_ref):
    tok, span = keep_ref.shape
    width = span - LANES
    rows = jnp.concatenate(ins, axis=0)
    total, tally = dot(place_ref[...], rows[:, :width]), dot(tally_ref[...], rows[:, width:])

    def fold(block):
        part = tally[block * QRY_DEV : (block + 1) * QRY_DEV]
        pieces = [part[:, i : i + LANES] for i in range(0, part.shape[1], LANES)]
        return jnp.concatenate(pieces, axis=0)

    keep_ref[:, :width] = total[:tok]
    keep_ref[:, width:] = fold(0)
    give_ref[:, :width] = total[tok:].astype(BF16)
    give_ref[:, width:] = fold(1).astype(BF16)


def guest_part_kernel(place_ref, tally_ref, *refs):
    token_sums(place_ref, tally_ref, [r[...] for r in refs[:-2]], *refs[-2:])


def own_part_kernel(deep, place_ref, tally_ref, rows_ref, keep_ref, give_ref):
    me = lax.axis_index("row") * deep + lax.axis_index("deep")
    ins = [rows_ref[i ^ me] for i in range(rows_ref.shape[0])]
    token_sums(place_ref, tally_ref, ins, keep_ref, give_ref)


def join_kernel(keep_ref, more_ref, out_ref):
    out_ref[...] = (keep_ref[...] + more_ref[...].astype(F32)).astype(BF16)


def final_kernel(keep_ref, more_ref, far_ref, grad_ref, score_ref):
    tok, width = grad_ref.shape
    total = keep_ref[...] + more_ref[...].astype(F32) + far_ref[...].astype(F32)
    grad_ref[...] = total[:, :width].astype(BF16)
    for i in range(tok // QRY_DEV):
        part = total[i * QRY_DEV : (i + 1) * QRY_DEV, width:]
        score_ref[:, i * LANES : (i + 1) * LANES] = part


VMEM = pl.BlockSpec(memory_space=pltpu.VMEM)
HBM = pl.BlockSpec(memory_space=pltpu.HBM)


def in_hbm(value):
    return pltpu.with_memory_space_constraint(value, pltpu.HBM)


def call(kernel, outs, in_specs, args, scratch=(), flops=1_000_000, moved=1_000_000, limit=8 << 20, out_specs=None):
    return pl.pallas_call(
        kernel,
        out_shape=outs,
        in_specs=in_specs,
        out_specs=out_specs or jax.tree.map(lambda _: VMEM, outs),
        scratch_shapes=scratch,
        compiler_params=pltpu.CompilerParams(vmem_limit_bytes=limit),
        cost_estimate=pl.CostEstimate(flops=flops, bytes_accessed=moved, transcendentals=0),
    )(*args)


def layer(tokens, out_grad, expert_ids, gate_w, query_ids, *weights):
    weights = weights[:3] + tuple(w.transpose(0, 2, 1) for w in weights[3:5]) + weights[5:]
    weights = tuple(in_hbm(w) for w in weights)
    tok, width = tokens.shape
    top = expert_ids.shape[1]
    experts = weights[0].shape[0]
    train = weights[5].shape[2]
    row_size, deep = lax.axis_size("row"), lax.axis_size("deep")
    chips = row_size * deep
    capacity = 2 * tok // (experts * PAIR * deep)
    piece = experts * PAIR * capacity
    shape = jax.ShapeDtypeStruct

    def swap(value, row=0, core=0, half=0, far=0):
        pairs = []
        for r in range(row_size):
            for c in range(PAIR):
                for h in range(PAIR):
                    for d in range(deep):
                        source = ((r * PAIR + c) * PAIR + h) * deep + d
                        target = (((r ^ row) * PAIR + (c ^ core)) * PAIR + (h ^ half)) * deep
                        pairs.append((source, target + (d ^ far)))
        return lax.ppermute(value, AXES, pairs)

    order = sorted(range(1, chips), key=lambda o: (-bin(o).count("1"), -o))

    def move(pieces, offsets):
        return {o: swap(pieces[o], row=o // deep, far=o % deep) for o in offsets}

    def exchange(pieces):
        moved = move(pieces, order)
        return [pieces[0]] + [moved[o] for o in range(1, chips)]

    def pack(first, second):
        outs = (shape((piece, 2 * width), BF16),) * chips
        outs += (shape((PAIR * tok, piece * chips), BF16),)
        outs += (shape((PAIR * QRY_DEV, piece * chips), BF16),)
        kernel = functools.partial(pack_kernel, top, experts, capacity, deep)
        filled = call(kernel, outs, [VMEM, VMEM], (first, second), limit=12 << 20)
        return filled[:-2], filled[-2:]

    inputs = tuple(in_hbm(v) for v in (expert_ids.T, gate_w.T, query_ids, tokens, out_grad))
    pay = call(
        pay_kernel,
        shape((tok, 2 * width + LANES), BF16),
        [HBM] * len(inputs),
        inputs,
        scratch=[pltpu.VMEM(v.shape, v.dtype) for v in inputs[:3]]
        + [pltpu.SemaphoreType.DMA((len(inputs),))],
    )
    guest = swap(pay, half=1)
    other = swap(pay, core=1)
    own_send, own_place = pack(pay, other)
    own_rows = exchange(own_send)
    other = swap(guest, core=1)
    guest_send, guest_place = pack(guest, other)
    guest_rows = exchange(guest_send)
    held = pl.pallas_call(
        load_kernel,
        out_shape=tuple(pltpu.VMEM(w.shape, w.dtype) for w in weights),
        in_specs=[HBM] * len(weights),
        out_specs=(VMEM,) * len(weights),
        scratch_shapes=[pltpu.SemaphoreType.DMA((len(weights),))],
        compiler_params=pltpu.CompilerParams(vmem_limit_bytes=1 << 20),
    )(*weights)
    rows = 2 * chips * piece
    size = sum(w.size for w in weights)
    outs = call(
        functools.partial(expert_kernel, 2 * chips, PAIR * capacity, deep),
        (shape((chips, piece, width + train), BF16),)
        + (shape((piece, width + train), BF16),) * chips,
        [VMEM] * (2 * chips + len(weights)),
        (*own_rows, *guest_rows, *held),
        scratch=[
            pltpu.VMEM((chips, piece, width + train), BF16),
            pltpu.VMEM((experts, rows // experts, weights[5].shape[1]), BF16),
            pltpu.SemaphoreType.DMA((2, chips)),
        ],
        out_specs=(HBM,) + (VMEM,) * chips,
        flops=2 * rows * size,
        moved=2 * size,
        limit=rows * (76 << 10),
    )
    assert QRY_DEV * train == tok * LANES
    guest_back = exchange(outs[1:])
    own_back = lax.all_to_all(outs[0], ("row", "deep"), 0, 0, tiled=True)
    sums = (shape((tok, width + LANES), F32), shape((tok, width + LANES), BF16))
    guest_keep, guest_give = call(
        guest_part_kernel, sums, [VMEM] * (2 + chips), (*guest_place, *guest_back)
    )
    more = swap(guest_give, core=1)
    far = call(join_kernel, sums[1], [VMEM] * 2, (guest_keep, more))
    far = swap(far, half=1)
    own_keep, own_give = call(
        functools.partial(own_part_kernel, deep),
        sums,
        [VMEM] * 3,
        (*own_place, own_back),
    )
    more = swap(own_give, core=1)
    return call(
        final_kernel,
        (shape((tok, width), BF16), shape((QRY_DEV, train), F32)),
        [VMEM] * 3,
        (own_keep, more, far),
    )


def solution(mesh):
    groups, line = mesh.shape["group"], mesh.shape["expert"]
    devices = mesh.devices.reshape(groups // PAIR, PAIR, PAIR, line // PAIR)
    return jax.shard_map(
        layer,
        mesh=Mesh(devices, AXES),
        in_specs=(P(AXES, None),) * 5 + (P(AXES, None, None),) * 6,
        out_specs=(P(AXES, None), P(AXES, None)),
        check_vma=False,
    )
```
